32 devices in a mesh: shots: 2 (over y), lat: 4 (over z), freq: 2 (over x), sub: 2 (over core).
Axes of the slice: x: 2, y: 2, z: 4, core: 2. Of those that a mesh axis runs over, the one named last changes fastest.
Arguments:
- wavefields: float32 [4, 4, 64, 1024], P(('shots', 'freq'), None, 'lat', 'sub'), parts along dimension 0, may hold values from -6 to 6
- velocity: float32 [8, 64, 1024], P('freq', 'lat', 'sub'), may hold values from 0 to 31
- filter_table: float32 [32, 32, 9, 2], replicated, may hold values from -1 to 1
- freq_pick: int32 [2], P('freq'), may hold values from 0 to 31
- slab_order: int32 [4], replicated, may hold values from 0 to 7
Outputs:
- fields_out: float32 [4, 4, 64, 1024], P(('shots', 'freq'), None, 'lat', 'sub'), parts along dimension 0
- image: float32 [8, 64, 1024], P(('shots', 'freq'), 'lat', 'sub'), parts along dimension 0
The draws below stay inside these ranges and needn't reach their ends.
There are 2 independent parts, one for each index of `shots`. The reference program is written for one: setup_inputs(seed, part) draws one part's arguments, and reference() takes and returns one part's arrays. A program takes and returns all parts, laid end to end along the dimension named above; an argument that names none is the same for every part. Nothing has to cross between parts.
All inputs are finite; a program needn't handle non-finite values.
Results may differ from the reference program's by a relative error of at most 0.0003.
Values sent between devices are 32-bit elements; how exact they have to be, the bound alone decides.
No kernel may reach another device: no remote copies, remote signals or barrier semaphores. Data moves between devices by JAX's collectives and lax.ppermute only.
A program may use at most 64 MiB of HBM per device.

```python
import jax
import jax.numpy as jnp
from jax import lax

DEPTHS = 4
KCHEB = 8
NBINS = 32
TABLE_FREQS = 32
STORED = 8
FREQS = 2
NX = 64
NY = 1024


def place_ends(result, stream_key, smallest, high):
    longest = result.shape.index(max(result.shape))
    spots = []
    for shift in (0, 1):
        where = [jax.random.randint(jax.random.fold_in(stream_key, axis), (), 0, length) for axis, length in enumerate(result.shape)]
        where[longest] = (where[longest] + shift) % result.shape[longest]
        spots.append(tuple(where))
    return result.at[spots[0]].set(smallest).at[spots[1]].set(high)


def steps_of(own_key, extent, split, smallest, top_value):
    def one(dim, shards_of):
        steps = jax.random.uniform(jax.random.fold_in(jax.random.fold_in(own_key, 6), dim), (shards_of,), jnp.float32, smallest / len(split), top_value / len(split))
        return jnp.repeat(jnp.exp(steps), extent[dim] // shards_of).reshape((-1,) + (1,) * (len(extent) - dim - 1))

    factor_of = one(*split[0])
    for cut in split[1:]:
        factor_of = factor_of * one(*cut)
    return factor_of


def centred(stream_key, shape, scale, reach, split=(), kind=jnp.bfloat16):
    values = jax.random.normal(stream_key, shape, jnp.float32) * scale
    if len(split) > 0:
        values = steps_of(stream_key, shape, split, -0.22, 0.18) * values
    return jnp.clip(values, min=-reach, max=reach).astype(kind)


def setup_inputs(seed: int = 0, part: int = 0) -> dict:
    arg_keys = jax.random.split(jax.random.key(seed), 6)
    part_keys = jax.random.split(jax.random.fold_in(arg_keys[5], part), 6)
    return {
        "wavefields": centred(part_keys[0], (FREQS, 4, NX, NY), 1.0, 6.0, ((0, 2), (2, 4), (3, 2)), jnp.float32),
        "velocity": jnp.clip(31.0 * jax.random.uniform(arg_keys[1], (STORED, NX, NY), jnp.float32) ** steps_of(arg_keys[1], (STORED, NX, NY), ((0, 2), (1, 4), (2, 2)), -0.2, 0.2), 0.0, 31.0),
        "filter_table": centred(arg_keys[2], (NBINS, TABLE_FREQS, KCHEB + 1, 2), 0.25, 1.0, (), jnp.float32),
        "freq_pick": jax.random.randint(arg_keys[3], (FREQS,), 0, TABLE_FREQS).astype(jnp.int32),
        "slab_order": place_ends(jax.random.randint(arg_keys[4], (DEPTHS,), 0, STORED), jax.random.fold_in(arg_keys[4], 1), 0, STORED - 1).astype(jnp.int32),
    }


def stencil(padded):
    edges = padded[:, :, 2:, 1:-1] + padded[:, :, :-2, 1:-1] + padded[:, :, 1:-1, 2:] + padded[:, :, 1:-1, :-2]
    corners = padded[:, :, 2:, 2:] + padded[:, :, 2:, :-2] + padded[:, :, :-2, 2:] + padded[:, :, :-2, :-2]
    return -0.5 * padded[:, :, 1:-1, 1:-1] + 0.25 * edges + 0.125 * corners


def operate(field):
    return stencil(jnp.pad(field, ((0, 0), (0, 0), (1, 1), (1, 1))))


def combine(pair, term):
    real_part = pair[:, 0][:, None]
    imag_part = pair[:, 1][:, None]
    turned = jnp.stack([term[:, 1], -term[:, 0], -term[:, 3], term[:, 2]], axis=1)
    return real_part * term + imag_part * turned


def reference(wavefields, velocity, filter_table, freq_pick, slab_order):
    highest = lax.Precision.HIGHEST
    onehot = (freq_pick[:, None] == jnp.arange(TABLE_FREQS, dtype=jnp.int32)[None, :]).astype(jnp.float32)
    selected = jnp.einsum("ft,btkc->bfkc", onehot, filter_table, precision=highest)
    selected = selected.reshape(NBINS, FREQS * (KCHEB + 1) * 2).T
    bin_grid = jnp.arange(NBINS, dtype=jnp.float32)[:, None]
    fields = wavefields
    images = []
    for depth_step in range(DEPTHS):
        slowness = velocity[slab_order[depth_step]]
        weights = jnp.maximum(0.0, 1.0 - jnp.abs(slowness.reshape(1, -1) - bin_grid))
        coefficients = jnp.dot(selected, weights, precision=highest, preferred_element_type=jnp.float32)
        coefficients = coefficients.reshape(FREQS, KCHEB + 1, 2, NX, NY)
        previous = fields
        summed = combine(coefficients[:, 0], previous)
        current = operate(previous)
        summed = summed + combine(coefficients[:, 1], current)
        for order in range(2, KCHEB + 1):
            following = 2.0 * operate(current) - previous
            previous, current = current, following
            summed = summed + combine(coefficients[:, order], current)
        fields = summed
        images.append(jnp.sum(fields[:, 0] * fields[:, 2] + fields[:, 1] * fields[:, 3], axis=0))
    return fields, jnp.stack(images)
```

```python
import functools

import jax
import jax.numpy as jnp
from jax import lax
from jax.experimental import pallas as pl
from jax.experimental.pallas import tpu as pltpu
from jax.sharding import PartitionSpec as P

PARTS = 4
LANES = 128
ROWS = 8


def lane_ids():
    return lax.broadcasted_iota(jnp.int32, (ROWS, LANES), 1)


def pick(tile, index):
    return jnp.take_along_axis(tile, index, axis=1)


def interleaved(natural):
    count = len(natural)
    lane = lane_ids()
    span = LANES // count
    home = lane // span
    tiles = []
    for j in range(count):
        index = count * (lane % span) + j
        out = pick(natural[0], index)
        for t in range(1, count):
            out = jnp.where(home == t, pick(natural[t], index), out)
        tiles.append(out)
    return tiles


def straightened(tiles):
    count = len(tiles)
    lane = lane_ids()
    home = lane % count
    natural = []
    for t in range(count):
        index = (LANES // count) * t + lane // count
        out = pick(tiles[0], index)
        for j in range(1, count):
            out = jnp.where(home == j, pick(tiles[j], index), out)
        natural.append(out)
    return natural


def chain_permutation(lat, freq):
    def flat(z, f, c):
        return (z * freq + f) * 2 + c

    pairs = []
    for f in range(freq):
        for z in range(lat - 1):
            pairs.append((flat(z, f, 1), flat(z + 1, f, 0)))
            pairs.append((flat(z + 1, f, 0), flat(z, f, 1)))
        if freq % 2 == 0:
            pairs.append((flat(0, f, 0), flat(0, f ^ 1, 0)))
            pairs.append((flat(lat - 1, f, 1), flat(lat - 1, f ^ 1, 1)))
    return pairs


SWAP = [(0, 1), (1, 0)]


def vmem(count):
    return [pl.BlockSpec(memory_space=pltpu.VMEM)] * count


def pack_fields(x_ref, other_ref, own_ref, mate_ref):
    core = lax.axis_index("sub")
    half = x_ref.shape[3] // LANES
    for target, row in ((own_ref, core), (mate_ref, 1 - core)):
        rows = pl.ds(pl.multiple_of(row * ROWS, ROWS), ROWS)
        for p in range(PARTS):
            mine = [x_ref[0, p, rows, t * LANES : (t + 1) * LANES] for t in range(half)]
            theirs = [other_ref[0, p, rows, t * LANES : (t + 1) * LANES] for t in range(half)]
            left = [jnp.where(core == 0, a, b) for a, b in zip(mine, theirs)]
            right = [jnp.where(core == 0, b, a) for a, b in zip(mine, theirs)]
            for j, tile in enumerate(interleaved(left + right)):
                target[p * 2 * half + j] = tile


def pack_velocity(order_ref, *refs):
    slabs, (keep_ref, send_ref) = refs[:-2], refs[-2:]
    core = lax.axis_index("sub")
    here = lax.axis_index("freq")
    count = len(slabs)
    size = slabs[0].shape[0]
    for d in range(keep_ref.shape[0]):
        stored = order_ref[d]
        slot = lax.rem(stored // size - here + count, count)
        local = lax.rem(stored, size)
        for target, row in ((keep_ref, core), (send_ref, 1 - core)):
            rows = pl.ds(pl.multiple_of(row * ROWS, ROWS), ROWS)
            value = slabs[0][local, rows, :]
            for s in range(1, count):
                value = jnp.where(slot == s, slabs[s][local, rows, :], value)
            target[d] = value


def chebyshev(terms, tiles, kcheb, up_scale, down_scale):
    lane = lane_ids()
    sub = lax.broadcasted_iota(jnp.int32, (ROWS, LANES), 0)
    first = lane == 0
    last = lane == LANES - 1
    half = ROWS // 2
    inside = jnp.full((ROWS, LANES), 0.25, jnp.float32)
    upper = jnp.where(sub < half, up_scale, inside)
    lower = jnp.where(sub >= half, down_scale, inside)
    own = 2 * ROWS
    for k in range(kcheb):
        reach = kcheb - (k + 1)
        if reach > half:
            windows = ((own - ROWS, up_scale), (own, inside), (own + ROWS, down_scale))
        elif reach > 0:
            windows = ((own - half, upper), (own + half, lower))
        else:
            windows = ((own, inside),)
        for row, scale in windows:
            for p in range(PARTS):
                base = p * tiles
                twice = []
                sums = []
                for j in range(tiles):
                    value = terms[k, base + j, pl.ds(row, ROWS), :]
                    double = value + value
                    around = terms[k, base + j, pl.ds(row - 1, ROWS), :] + terms[k, base + j, pl.ds(row + 1, ROWS), :]
                    sums.append(around + double)
                    twice.append(value if k == 0 else double)
                before = jnp.where(first, 0.0, pltpu.roll(sums[tiles - 1], 1, 1))
                after = jnp.where(last, 0.0, pltpu.roll(sums[0], LANES - 1, 1))
                pair = [sums[j] + sums[j + 1] for j in range(tiles - 1)]
                full = [pair[0] + (sums[0] + before)]
                full += [pair[j - 1] + pair[j] for j in range(1, tiles - 1)]
                full.append(pair[tiles - 2] + (sums[tiles - 1] + after))
                for j in range(tiles):
                    if k == 0:
                        new = (0.5 * scale) * full[j] - twice[j]
                    else:
                        new = scale * full[j] - (twice[j] + terms[k - 1, base + j, pl.ds(row, ROWS), :])
                    terms[k + 1, base + j, pl.ds(row, ROWS), :] = new


def combined(terms, velocity, table, tiles, kcheb, bins):
    own = 2 * ROWS
    out = []
    for j in range(tiles):
        v = velocity[j]
        low = jnp.clip(v.astype(jnp.int32), 0, bins - 1)
        part = v - low.astype(jnp.float32)
        total = [None] * PARTS
        for k in range(kcheb + 1):
            a, b = [
                pick(table[0, 2 * k + c], low) + part * pick(table[1, 2 * k + c], low) for c in range(2)
            ]
            sr, si, rr, ri = [terms[k, p * tiles + j, pl.ds(own, ROWS), :] for p in range(PARTS)]
            adds = (a * sr + b * si, a * si - b * sr, a * rr - b * ri, a * ri + b * rr)
            total = [x if y is None else y + x for x, y in zip(adds, total)]
        out.append((total, total[0] * total[2] + total[1] * total[3]))
    return out


def depth_step(depth, kcheb, bins, final, table_ref, keep_ref, other_ref, own_ref, mate_ref, zmate_ref, *refs):
    core = lax.axis_index("sub")
    block = lax.axis_index("lat") * 2 + core
    blocks = 2 * lax.axis_size("lat")
    tiles = own_ref.shape[0] // PARTS
    half = tiles // 2
    if final:
        past, refs = refs[: depth], refs[depth:]
        kept_ref, sub_ref, here_ref, cross_ref, terms, table = refs
    else:
        new_ref, image_ref, terms, table = refs
    own = 2 * ROWS
    up_ok = block > 0
    down_ok = block < blocks - 1
    for i in range(PARTS * tiles):
        terms[0, i, pl.ds(own, ROWS), :] = own_ref[i]
        a = mate_ref[i]
        b = zmate_ref[i]
        terms[0, i, pl.ds(own - ROWS, ROWS), :] = jnp.where(up_ok, jnp.where(core == 0, b, a), 0.0)
        terms[0, i, pl.ds(own + ROWS, ROWS), :] = jnp.where(down_ok, jnp.where(core == 0, a, b), 0.0)
    low = table_ref[...]
    step = pltpu.roll(low, LANES - 1, 1) - low
    for i in range(2 * (kcheb + 1)):
        table[0, i] = jnp.broadcast_to(low[i : i + 1], (ROWS, LANES))
        table[1, i] = jnp.broadcast_to(step[i : i + 1], (ROWS, LANES))
    mine = [keep_ref[depth, :, t * LANES : (t + 1) * LANES] for t in range(half)]
    theirs = [other_ref[depth, :, t * LANES : (t + 1) * LANES] for t in range(half)]
    left = [jnp.where(core == 0, a, b) for a, b in zip(mine, theirs)]
    right = [jnp.where(core == 0, b, a) for a, b in zip(mine, theirs)]
    velocity = interleaved(left + right)

    shape = (ROWS, LANES)
    up_scale = jnp.where(up_ok, jnp.full(shape, 0.25, jnp.float32), 0.0)
    down_scale = jnp.where(down_ok, jnp.full(shape, 0.25, jnp.float32), 0.0)
    chebyshev(terms, tiles, kcheb, up_scale, down_scale)
    result = combined(terms, velocity, table, tiles, kcheb, bins)

    if not final:
        for j, (total, image) in enumerate(result):
            for p in range(PARTS):
                new_ref[p * tiles + j] = total[p]
            image_ref[j] = image
        return
    depths = depth + 1
    owners = lax.axis_size("freq")
    each = depths // owners
    here = lax.axis_index("freq")

    def halves(stack):
        natural = straightened(stack)
        left, right = natural[:half], natural[half:]
        mine = [jnp.where(core == 0, a, b) for a, b in zip(left, right)]
        theirs = [jnp.where(core == 0, b, a) for a, b in zip(left, right)]
        return jnp.concatenate(mine, axis=1), jnp.concatenate(theirs, axis=1)

    for p in range(PARTS):
        mine, theirs = halves([result[j][0][p] for j in range(tiles)])
        kept_ref[p] = mine
        sub_ref[p] = theirs
    for d in range(depths):
        stack = [result[j][1] for j in range(tiles)] if d == depth else [past[d][j] for j in range(tiles)]
        mine, theirs = halves(stack)
        shift = lax.rem(d // each - here + owners, owners)
        slot = d % each

        @pl.when(shift == 0)
        def _():
            kept_ref[PARTS + slot] = mine
            sub_ref[PARTS + slot] = theirs

        @pl.when(shift != 0)
        def _():
            here_ref[shift - 1, slot] = mine
            cross_ref[shift - 1, slot] = theirs


def assemble(kept_ref, sub_ref, *refs):
    pairs, (fields_ref, image_ref) = refs[:-2], refs[-2:]
    core = lax.axis_index("sub")
    each = image_ref.shape[0]
    mine = pl.ds(pl.multiple_of(core * ROWS, ROWS), ROWS)
    theirs = pl.ds(pl.multiple_of((1 - core) * ROWS, ROWS), ROWS)
    for p in range(PARTS):
        fields_ref[0, p, mine, :] = kept_ref[p]
        fields_ref[0, p, theirs, :] = sub_ref[p]
    for d in range(each):
        image_ref[d, mine, :] = functools.reduce(jnp.add, [r[d] for r in pairs[0::2]], kept_ref[PARTS + d])
        image_ref[d, theirs, :] = functools.reduce(jnp.add, [r[d] for r in pairs[1::2]], sub_ref[PARTS + d])


def body(wavefields, velocity, filter_table, freq_pick, slab_order):
    f32 = jnp.float32
    lat = lax.axis_size("lat")
    freq = lax.axis_size("freq")
    bins, _, terms, _ = filter_table.shape
    kcheb = terms - 1
    _, parts, rows, cols = wavefields.shape
    depths = slab_order.shape[0]
    tiles = 2 * cols // LANES
    each = depths // freq
    assert rows == 2 * ROWS and kcheb == ROWS and parts == PARTS and lax.axis_size("sub") == 2

    slabs = [velocity]
    for s in range(1, freq):
        slabs.append(lax.ppermute(velocity, "freq", [((i + s) % freq, i) for i in range(freq)]))
    other = lax.ppermute(wavefields, "sub", SWAP)

    table = lax.dynamic_index_in_dim(filter_table, freq_pick[0], 1, keepdims=False)
    table = table.reshape(bins, 2 * terms).T
    table = jnp.pad(table, ((0, 0), (0, LANES - bins)))

    block = jax.ShapeDtypeStruct((PARTS * tiles, ROWS, LANES), f32)
    own, mate = pl.pallas_call(
        pack_fields, out_shape=(block, block), in_specs=vmem(2), out_specs=tuple(vmem(2)), name="pack_fields"
    )(wavefields, other)
    chain = chain_permutation(lat, freq)
    axes = ("lat", "freq", "sub")
    zmate = lax.ppermute(own, axes, chain)

    strip = jax.ShapeDtypeStruct((depths, ROWS, cols), f32)
    keep, send = pl.pallas_call(
        pack_velocity,
        out_shape=(strip, strip),
        in_specs=[pl.BlockSpec(memory_space=pltpu.SMEM)] + vmem(freq),
        out_specs=tuple(vmem(2)),
        name="pack_velocity",
    )(slab_order, *slabs)
    theirs = lax.ppermute(send, "sub", SWAP)

    scratch = [
        pltpu.VMEM((terms, PARTS * tiles, 5 * ROWS, LANES), f32),
        pltpu.VMEM((2, 2 * terms, ROWS, LANES), f32),
    ]
    images = []
    for depth in range(depths):
        final = depth == depths - 1
        if final:
            out_shape = (
                jax.ShapeDtypeStruct((PARTS + each, ROWS, cols), f32),
                jax.ShapeDtypeStruct((PARTS + each, ROWS, cols), f32),
                jax.ShapeDtypeStruct((freq - 1, each, ROWS, cols), f32),
                jax.ShapeDtypeStruct((freq - 1, each, ROWS, cols), f32),
            )
        else:
            out_shape = (block, jax.ShapeDtypeStruct((tiles, ROWS, LANES), f32))
        args = (table, keep, theirs, own, mate, zmate) + (tuple(images) if final else ())
        out = pl.pallas_call(
            functools.partial(depth_step, depth, kcheb, bins, final),
            out_shape=out_shape,
            in_specs=vmem(len(args)),
            out_specs=tuple(vmem(len(out_shape))),
            scratch_shapes=scratch,
            name="last_step" if final else "depth_step",
        )(*args)
        if not final:
            own, image = out
            images.append(image)
            zmate = lax.ppermute(own, axes, chain)
            mate = lax.ppermute(own, "sub", SWAP)

    kept, sub_send, here_send, cross_send = out
    sub_got = lax.ppermute(sub_send, "sub", SWAP)
    pairs = []
    for s in range(1, freq):
        pairs.append(lax.ppermute(here_send[s - 1], "freq", [(i, (i + s) % freq) for i in range(freq)]))
        cross = [(2 * i + c, 2 * ((i + s) % freq) + 1 - c) for i in range(freq) for c in range(2)]
        pairs.append(lax.ppermute(cross_send[s - 1], ("freq", "sub"), cross))
    return pl.pallas_call(
        assemble,
        out_shape=(
            jax.ShapeDtypeStruct(wavefields.shape, f32),
            jax.ShapeDtypeStruct((each, rows, cols), f32),
        ),
        in_specs=vmem(2 + len(pairs)),
        out_specs=tuple(vmem(2)),
        name="assemble",
    )(kept, sub_got, *pairs)


def solution(mesh):
    return jax.shard_map(
        body,
        mesh=mesh,
        in_specs=(
            P(("shots", "freq"), None, "lat", "sub"),
            P("freq", "lat", "sub"),
            P(),
            P("freq"),
            P(),
        ),
        out_specs=(P(("shots", "freq"), None, "lat", "sub"), P(("shots", "freq"), "lat", "sub")),
        check_vma=False,
    )
```

```python
import functools

import jax
import jax.numpy as jnp
from jax import lax
from jax.experimental import pallas as pl
from jax.experimental.pallas import tpu as pltpu
from jax.sharding import PartitionSpec as P

PARTS = 4
LANES = 128
ROWS = 8


def lane_ids():
    return lax.broadcasted_iota(jnp.int32, (ROWS, LANES), 1)


def pick(tile, index):
    return jnp.take_along_axis(tile, index, axis=1)


def interleaved(natural):
    count = len(natural)
    lane = lane_ids()
    span = LANES // count
    home = lane // span
    tiles = []
    for j in range(count):
        index = count * (lane % span) + j
        out = pick(natural[0], index)
        for t in range(1, count):
            out = jnp.where(home == t, pick(natural[t], index), out)
        tiles.append(out)
    return tiles


def straightened(tiles):
    count = len(tiles)
    lane = lane_ids()
    home = lane % count
    natural = []
    for t in range(count):
        index = (LANES // count) * t + lane // count
        out = pick(tiles[0], index)
        for j in range(1, count):
            out = jnp.where(home == j, pick(tiles[j], index), out)
        natural.append(out)
    return natural


def chain_permutation(lat, freq):
    def flat(z, f, c):
        return (z * freq + f) * 2 + c

    pairs = []
    for f in range(freq):
        for z in range(lat - 1):
            pairs.append((flat(z, f, 1), flat(z + 1, f, 0)))
            pairs.append((flat(z + 1, f, 0), flat(z, f, 1)))
        if freq % 2 == 0:
            pairs.append((flat(0, f, 0), flat(0, f ^ 1, 0)))
            pairs.append((flat(lat - 1, f, 1), flat(lat - 1, f ^ 1, 1)))
    return pairs


SWAP = [(0, 1), (1, 0)]
SMALL = pltpu.CompilerParams(vmem_limit_bytes=4 << 20)
STEP = pltpu.CompilerParams(vmem_limit_bytes=12 << 20)


def vmem(count):
    return [pl.BlockSpec(memory_space=pltpu.VMEM)] * count


def pack_fields(x_ref, other_ref, own_ref, mate_ref):
    core = lax.axis_index("sub")
    half = x_ref.shape[3] // LANES
    for target, row in ((own_ref, core), (mate_ref, 1 - core)):
        rows = pl.ds(pl.multiple_of(row * ROWS, ROWS), ROWS)
        for p in range(PARTS):
            mine = [x_ref[0, p, rows, t * LANES : (t + 1) * LANES] for t in range(half)]
            theirs = [other_ref[0, p, rows, t * LANES : (t + 1) * LANES] for t in range(half)]
            left = [jnp.where(core == 0, a, b) for a, b in zip(mine, theirs)]
            right = [jnp.where(core == 0, b, a) for a, b in zip(mine, theirs)]
            for j, tile in enumerate(interleaved(left + right)):
                target[p * 2 * half + j] = tile


def pack_velocity(order_ref, *refs):
    slabs, (keep_ref, send_ref) = refs[:-2], refs[-2:]
    core = lax.axis_index("sub")
    here = lax.axis_index("freq")
    count = len(slabs)
    size = slabs[0].shape[0]
    for d in range(keep_ref.shape[0]):
        stored = order_ref[d]
        slot = lax.rem(stored // size - here + count, count)
        local = lax.rem(stored, size)
        for target, row in ((keep_ref, core), (send_ref, 1 - core)):
            rows = pl.ds(pl.multiple_of(row * ROWS, ROWS), ROWS)
            value = slabs[0][local, rows, :]
            for s in range(1, count):
                value = jnp.where(slot == s, slabs[s][local, rows, :], value)
            target[d] = value


def chebyshev(terms, tiles, kcheb, up_scale, down_scale):
    lane = lane_ids()
    sub = lax.broadcasted_iota(jnp.int32, (ROWS, LANES), 0)
    first = lane == 0
    last = lane == LANES - 1
    half = ROWS // 2
    inside = jnp.full((ROWS, LANES), 0.25, jnp.float32)
    upper = jnp.where(sub < half, up_scale, inside)
    lower = jnp.where(sub >= half, down_scale, inside)
    own = 2 * ROWS
    for k in range(kcheb):
        reach = kcheb - (k + 1)
        if reach > half:
            windows = ((own - ROWS, up_scale), (own, inside), (own + ROWS, down_scale))
        elif reach > 0:
            windows = ((own - half, upper), (own + half, lower))
        else:
            windows = ((own, inside),)
        for row, scale in windows:
            for p in range(PARTS):
                base = p * tiles
                twice = []
                sums = []
                for j in range(tiles):
                    value = terms[k, base + j, pl.ds(row, ROWS), :]
                    double = value + value
                    around = terms[k, base + j, pl.ds(row - 1, ROWS), :] + terms[k, base + j, pl.ds(row + 1, ROWS), :]
                    sums.append(around + double)
                    twice.append(value if k == 0 else double)
                before = jnp.where(first, 0.0, pltpu.roll(sums[tiles - 1], 1, 1))
                after = jnp.where(last, 0.0, pltpu.roll(sums[0], LANES - 1, 1))
                pair = [sums[j] + sums[j + 1] for j in range(tiles - 1)]
                full = [pair[0] + (sums[0] + before)]
                full += [pair[j - 1] + pair[j] for j in range(1, tiles - 1)]
                full.append(pair[tiles - 2] + (sums[tiles - 1] + after))
                for j in range(tiles):
                    if k == 0:
                        new = (0.5 * scale) * full[j] - twice[j]
                    else:
                        new = scale * full[j] - (twice[j] + terms[k - 1, base + j, pl.ds(row, ROWS), :])
                    terms[k + 1, base + j, pl.ds(row, ROWS), :] = new


def combined(terms, velocity, table, tiles, kcheb, bins):
    own = 2 * ROWS
    out = []
    for j in range(tiles):
        v = velocity[j]
        low = jnp.clip(v.astype(jnp.int32), 0, bins - 1)
        part = v - low.astype(jnp.float32)
        total = [None] * PARTS
        for k in range(kcheb + 1):
            a, b = [
                pick(table[0, 2 * k + c], low) + part * pick(table[1, 2 * k + c], low) for c in range(2)
            ]
            sr, si, rr, ri = [terms[k, p * tiles + j, pl.ds(own, ROWS), :] for p in range(PARTS)]
            adds = (a * sr + b * si, a * si - b * sr, a * rr - b * ri, a * ri + b * rr)
            total = [x if y is None else y + x for x, y in zip(adds, total)]
        out.append((total, total[0] * total[2] + total[1] * total[3]))
    return out


def depth_step(depth, kcheb, bins, final, table_ref, keep_ref, other_ref, own_ref, mate_ref, zmate_ref, *refs):
    core = lax.axis_index("sub")
    block = lax.axis_index("lat") * 2 + core
    blocks = 2 * lax.axis_size("lat")
    tiles = own_ref.shape[0] // PARTS
    half = tiles // 2
    if final:
        past, refs = refs[: depth], refs[depth:]
        kept_ref, sub_ref, here_ref, cross_ref, terms, table = refs
    else:
        new_ref, image_ref, terms, table = refs
    own = 2 * ROWS
    up_ok = block > 0
    down_ok = block < blocks - 1
    for i in range(PARTS * tiles):
        terms[0, i, pl.ds(own, ROWS), :] = own_ref[i]
        a = mate_ref[i]
        b = zmate_ref[i]
        terms[0, i, pl.ds(own - ROWS, ROWS), :] = jnp.where(up_ok, jnp.where(core == 0, b, a), 0.0)
        terms[0, i, pl.ds(own + ROWS, ROWS), :] = jnp.where(down_ok, jnp.where(core == 0, a, b), 0.0)
    low = table_ref[...]
    step = pltpu.roll(low, LANES - 1, 1) - low
    for i in range(2 * (kcheb + 1)):
        table[0, i] = jnp.broadcast_to(low[i : i + 1], (ROWS, LANES))
        table[1, i] = jnp.broadcast_to(step[i : i + 1], (ROWS, LANES))
    mine = [keep_ref[depth, :, t * LANES : (t + 1) * LANES] for t in range(half)]
    theirs = [other_ref[depth, :, t * LANES : (t + 1) * LANES] for t in range(half)]
    left = [jnp.where(core == 0, a, b) for a, b in zip(mine, theirs)]
    right = [jnp.where(core == 0, b, a) for a, b in zip(mine, theirs)]
    velocity = interleaved(left + right)

    shape = (ROWS, LANES)
    up_scale = jnp.where(up_ok, jnp.full(shape, 0.25, jnp.float32), 0.0)
    down_scale = jnp.where(down_ok, jnp.full(shape, 0.25, jnp.float32), 0.0)
    chebyshev(terms, tiles, kcheb, up_scale, down_scale)
    result = combined(terms, velocity, table, tiles, kcheb, bins)

    if not final:
        for j, (total, image) in enumerate(result):
            for p in range(PARTS):
                new_ref[p * tiles + j] = total[p]
            image_ref[j] = image
        return
    depths = depth + 1
    owners = lax.axis_size("freq")
    each = depths // owners
    here = lax.axis_index("freq")

    def halves(stack):
        natural = straightened(stack)
        left, right = natural[:half], natural[half:]
        mine = [jnp.where(core == 0, a, b) for a, b in zip(left, right)]
        theirs = [jnp.where(core == 0, b, a) for a, b in zip(left, right)]
        return jnp.concatenate(mine, axis=1), jnp.concatenate(theirs, axis=1)

    for p in range(PARTS):
        mine, theirs = halves([result[j][0][p] for j in range(tiles)])
        kept_ref[p] = mine
        sub_ref[p] = theirs
    for d in range(depths):
        stack = [result[j][1] for j in range(tiles)] if d == depth else [past[d][j] for j in range(tiles)]
        mine, theirs = halves(stack)
        shift = lax.rem(d // each - here + owners, owners)
        slot = d % each

        @pl.when(shift == 0)
        def _():
            kept_ref[PARTS + slot] = mine
            sub_ref[PARTS + slot] = theirs

        @pl.when(shift != 0)
        def _():
            here_ref[shift - 1, slot] = mine
            cross_ref[shift - 1, slot] = theirs


def assemble(kept_ref, sub_ref, *refs):
    pairs, (fields_ref, image_ref) = refs[:-2], refs[-2:]
    core = lax.axis_index("sub")
    each = image_ref.shape[0]
    mine = pl.ds(pl.multiple_of(core * ROWS, ROWS), ROWS)
    theirs = pl.ds(pl.multiple_of((1 - core) * ROWS, ROWS), ROWS)
    for p in range(PARTS):
        fields_ref[0, p, mine, :] = kept_ref[p]
        fields_ref[0, p, theirs, :] = sub_ref[p]
    for d in range(each):
        image_ref[d, mine, :] = functools.reduce(jnp.add, [r[d] for r in pairs[0::2]], kept_ref[PARTS + d])
        image_ref[d, theirs, :] = functools.reduce(jnp.add, [r[d] for r in pairs[1::2]], sub_ref[PARTS + d])


def body(wavefields, velocity, filter_table, freq_pick, slab_order):
    f32 = jnp.float32
    lat = lax.axis_size("lat")
    freq = lax.axis_size("freq")
    bins, _, terms, _ = filter_table.shape
    kcheb = terms - 1
    _, parts, rows, cols = wavefields.shape
    depths = slab_order.shape[0]
    tiles = 2 * cols // LANES
    each = depths // freq
    assert rows == 2 * ROWS and kcheb == ROWS and parts == PARTS and lax.axis_size("sub") == 2

    slabs = [velocity]
    for s in range(1, freq):
        slabs.append(lax.ppermute(velocity, "freq", [((i + s) % freq, i) for i in range(freq)]))
    other = lax.ppermute(wavefields, "sub", SWAP)

    table = lax.dynamic_index_in_dim(filter_table, freq_pick[0], 1, keepdims=False)
    table = table.reshape(bins, 2 * terms).T
    table = jnp.pad(table, ((0, 0), (0, LANES - bins)))

    block = jax.ShapeDtypeStruct((PARTS * tiles, ROWS, LANES), f32)
    own, mate = pl.pallas_call(
        pack_fields, out_shape=(block, block), in_specs=vmem(2), out_specs=tuple(vmem(2)), compiler_params=SMALL,
        name="pack_fields",
    )(wavefields, other)
    chain = chain_permutation(lat, freq)
    axes = ("lat", "freq", "sub")
    zmate = lax.ppermute(own, axes, chain)

    strip = jax.ShapeDtypeStruct((depths, ROWS, cols), f32)
    keep, send = pl.pallas_call(
        pack_velocity,
        out_shape=(strip, strip),
        in_specs=[pl.BlockSpec(memory_space=pltpu.SMEM)] + vmem(freq),
        out_specs=tuple(vmem(2)),
        compiler_params=SMALL,
        name="pack_velocity",
    )(slab_order, *slabs)
    theirs = lax.ppermute(send, "sub", SWAP)

    scratch = [
        pltpu.VMEM((terms, PARTS * tiles, 5 * ROWS, LANES), f32),
        pltpu.VMEM((2, 2 * terms, ROWS, LANES), f32),
    ]
    images = []
    for depth in range(depths):
        final = depth == depths - 1
        if final:
            out_shape = (
                jax.ShapeDtypeStruct((PARTS + each, ROWS, cols), f32),
                jax.ShapeDtypeStruct((PARTS + each, ROWS, cols), f32),
                jax.ShapeDtypeStruct((freq - 1, each, ROWS, cols), f32),
                jax.ShapeDtypeStruct((freq - 1, each, ROWS, cols), f32),
            )
        else:
            out_shape = (block, jax.ShapeDtypeStruct((tiles, ROWS, LANES), f32))
        args = (table, keep, theirs, own, mate, zmate) + (tuple(images) if final else ())
        out = pl.pallas_call(
            functools.partial(depth_step, depth, kcheb, bins, final),
            out_shape=out_shape,
            in_specs=vmem(len(args)),
            out_specs=tuple(vmem(len(out_shape))),
            scratch_shapes=scratch,
            compiler_params=STEP,
            name="last_step" if final else "depth_step",
        )(*args)
        if not final:
            own, image = out
            images.append(image)
            zmate = lax.ppermute(own, axes, chain)
            mate = lax.ppermute(own, "sub", SWAP)

    kept, sub_send, here_send, cross_send = out
    sub_got = lax.ppermute(sub_send, "sub", SWAP)
    pairs = []
    for s in range(1, freq):
        pairs.append(lax.ppermute(here_send[s - 1], "freq", [(i, (i + s) % freq) for i in range(freq)]))
        cross = [(2 * i + c, 2 * ((i + s) % freq) + 1 - c) for i in range(freq) for c in range(2)]
        pairs.append(lax.ppermute(cross_send[s - 1], ("freq", "sub"), cross))
    return pl.pallas_call(
        assemble,
        out_shape=(
            jax.ShapeDtypeStruct(wavefields.shape, f32),
            jax.ShapeDtypeStruct((each, rows, cols), f32),
        ),
        in_specs=vmem(2 + len(pairs)),
        out_specs=tuple(vmem(2)),
        compiler_params=SMALL,
        name="assemble",
    )(kept, sub_got, *pairs)


def solution(mesh):
    return jax.shard_map(
        body,
        mesh=mesh,
        in_specs=(
            P(("shots", "freq"), None, "lat", "sub"),
            P("freq", "lat", "sub"),
            P(),
            P("freq"),
            P(),
        ),
        out_specs=(P(("shots", "freq"), None, "lat", "sub"), P(("shots", "freq"), "lat", "sub")),
        check_vma=False,
    )
```

```python
import functools

import jax
import jax.numpy as jnp
from jax import lax
from jax.experimental import pallas as pl
from jax.experimental.pallas import tpu as pltpu
from jax.sharding import PartitionSpec as P


PARTS = 4
LANES = 128
ROWS = 8


def lane_ids():
    return lax.broadcasted_iota(jnp.int32, (ROWS, LANES), 1)


def pick(tile, index):
    return jnp.take_along_axis(tile, index, axis=1)


def straightened(tiles):
    count = len(tiles)
    lane = lane_ids()
    home = lane % count
    natural = []
    for t in range(count):
        index = (LANES // count) * t + lane // count
        out = pick(tiles[0], index)
        for j in range(1, count):
            out = jnp.where(home == j, pick(tiles[j], index), out)
        natural.append(out)
    return natural


def chain_permutation(lat, freq):
    def flat(z, f, c):
        return (z * freq + f) * 2 + c

    pairs = []
    for f in range(freq):
        for z in range(lat - 1):
            pairs.append((flat(z, f, 1), flat(z + 1, f, 0)))
            pairs.append((flat(z + 1, f, 0), flat(z, f, 1)))
        if freq % 2 == 0:
            pairs.append((flat(0, f, 0), flat(0, f ^ 1, 0)))
            pairs.append((flat(lat - 1, f, 1), flat(lat - 1, f ^ 1, 1)))
    return pairs


SWAP = [(0, 1), (1, 0)]
SMALL = pltpu.CompilerParams(vmem_limit_bytes=4 << 20)
STEP = pltpu.CompilerParams(vmem_limit_bytes=12 << 20)


def vmem(count):
    return [pl.BlockSpec(memory_space=pltpu.VMEM)] * count


def cost(flops):
    return pl.CostEstimate(flops=flops, bytes_accessed=1 << 16, transcendentals=0)


def spread_half(natural, core, out, tiles):
    lane = lane_ids()
    span = LANES // tiles
    home = lane // span - core * (tiles // 2)
    result = []
    for j in range(tiles):
        index = tiles * (lane % span) + j
        value = out[j]
        for t, tile in enumerate(natural):
            got = pick(tile, index)
            value = got if value is None else jnp.where(home == t, got, value)
        result.append(value)
    return result


def compacted(natural):
    half = len(natural)
    lane = lane_ids()
    within = lane % (LANES // 2)
    span = LANES // (2 * half)
    home = within // span
    tiles = []
    for i in range(half):
        index = 2 * half * (within % span) + i + half * (lane // (LANES // 2))
        value = pick(natural[0], index)
        for t in range(1, half):
            value = jnp.where(home == t, pick(natural[t], index), value)
        tiles.append(value)
    return tiles


def merged(left, right):
    middle = LANES // 2
    low = lane_ids() < middle
    first = [jnp.where(low, a, pltpu.roll(b, middle, 1)) for a, b in zip(left, right)]
    second = [jnp.where(low, pltpu.roll(a, middle, 1), b) for a, b in zip(left, right)]
    return first + second


def arrange_fields(x_ref, own_ref, mate_ref):
    half = x_ref.shape[3] // LANES
    for target, rows in zip((own_ref, mate_ref), both_rows()):
        for p in range(PARTS):
            natural = [x_ref[0, p, rows, t * LANES : (t + 1) * LANES] for t in range(half)]
            for i, tile in enumerate(compacted(natural)):
                target[p * half + i] = tile


def pack_velocity(order_ref, *refs):
    slabs, (keep_ref, send_ref) = refs[:-2], refs[-2:]
    core = lax.axis_index("sub")
    here = lax.axis_index("freq")
    count = len(slabs)
    size = slabs[0].shape[0]
    half = keep_ref.shape[2] // LANES
    for target, row in ((keep_ref, core), (send_ref, 1 - core)):
        rows = pl.ds(pl.multiple_of(row * ROWS, ROWS), ROWS)
        for t in range(half):
            columns = slice(t * LANES, (t + 1) * LANES)
            values = [[slabs[s][i, rows, columns] for i in range(size)] for s in range(count)]
            for d in range(keep_ref.shape[0]):
                stored = order_ref[d]
                value = values[0][0]
                for s in range(count):
                    first = lax.rem(here + s, count) * size
                    for i in range(size):
                        if s or i:
                            value = jnp.where(stored == first + i, values[s][i], value)
                target[d, :, columns] = value


def chebyshev(terms, tiles, kcheb, up_scale, down_scale):
    lane = lane_ids()
    sub = lax.broadcasted_iota(jnp.int32, (ROWS, LANES), 0)
    first = lane == 0
    last = lane == LANES - 1
    half = ROWS // 2
    inside = jnp.full((ROWS, LANES), 0.25, jnp.float32)
    upper = jnp.where(sub < half, up_scale, inside)
    lower = jnp.where(sub >= half, down_scale, inside)
    own = 2 * ROWS
    for k in range(kcheb):
        reach = kcheb - (k + 1)
        if reach > half:
            windows = ((own - ROWS, up_scale), (own, inside), (own + ROWS, down_scale))
        elif reach > 0:
            windows = ((own - half, upper), (own + half, lower))
        else:
            windows = ((own, inside),)
        for row, scale in windows:
            for p in range(PARTS):
                base = p * tiles
                twice = []
                sums = []
                for j in range(tiles):
                    value = terms[k, base + j, pl.ds(row, ROWS), :]
                    double = value + value
                    around = terms[k, base + j, pl.ds(row - 1, ROWS), :] + terms[k, base + j, pl.ds(row + 1, ROWS), :]
                    sums.append(around + double)
                    twice.append(value if k == 0 else double)
                before = jnp.where(first, 0.0, pltpu.roll(sums[tiles - 1], 1, 1))
                after = jnp.where(last, 0.0, pltpu.roll(sums[0], LANES - 1, 1))
                pair = [sums[j] + sums[j + 1] for j in range(tiles - 1)]
                full = [pair[0] + (sums[0] + before)]
                full += [pair[j - 1] + pair[j] for j in range(1, tiles - 1)]
                full.append(pair[tiles - 2] + (sums[tiles - 1] + after))
                for j in range(tiles):
                    if k == 0:
                        new = (0.5 * scale) * full[j] - twice[j]
                    else:
                        new = scale * full[j] - (twice[j] + terms[k - 1, base + j, pl.ds(row, ROWS), :])
                    terms[k + 1, base + j, pl.ds(row, ROWS), :] = new


def coefficients(depth, bins, table_ref, keep_ref, other_ref, *refs):
    out_ref = refs[-1]
    core = lax.axis_index("sub")
    count, tiles = out_ref.shape[:2]
    half = tiles // 2
    velocity = [None] * tiles
    for ref, home in ((keep_ref, core), (other_ref, 1 - core)):
        strips = [ref[depth, :, t * LANES : (t + 1) * LANES] for t in range(half)]
        velocity = spread_half(strips, home, velocity, tiles)
    lows = [jnp.clip(v.astype(jnp.int32), 0, bins - 1) for v in velocity]
    parts = [v - low.astype(jnp.float32) for v, low in zip(velocity, lows)]
    table = table_ref[...]
    step = pltpu.roll(table, LANES - 1, 1) - table
    for i in range(count):
        at_low = jnp.broadcast_to(table[i : i + 1], (ROWS, LANES))
        rise = jnp.broadcast_to(step[i : i + 1], (ROWS, LANES))
        for j in range(tiles):
            out_ref[i, j] = pick(at_low, lows[j]) + parts[j] * pick(rise, lows[j])


def combined(terms, coefficient, j, tiles, kcheb):
    own = 2 * ROWS
    total = None
    for k in range(kcheb + 1):
        a = coefficient[2 * k, j]
        b = coefficient[2 * k + 1, j]
        sr, si, rr, ri = [terms[k, p * tiles + j, pl.ds(own, ROWS), :] for p in range(PARTS)]
        adds = (a * sr + b * si, a * si - b * sr, a * rr - b * ri, a * ri + b * rr)
        total = adds if total is None else tuple(y + x for x, y in zip(adds, total))
    return total


def halves(stack, core):
    natural = straightened(stack)
    half = len(natural) // 2
    left, right = natural[:half], natural[half:]
    mine = [jnp.where(core == 0, a, b) for a, b in zip(left, right)]
    theirs = [jnp.where(core == 0, b, a) for a, b in zip(left, right)]
    return jnp.concatenate(mine, axis=1), jnp.concatenate(theirs, axis=1)


def whole_blocks(refs):
    core = lax.axis_index("sub")
    half = refs[0].shape[0] // PARTS
    blocks = []
    for ours, others in (refs[0:2], refs[2:4], refs[4:6]):
        tiles = []
        for p in range(PARTS):
            a = [ours[p * half + i] for i in range(half)]
            b = [others[p * half + i] for i in range(half)]
            left = [jnp.where(core == 0, x, y) for x, y in zip(a, b)]
            right = [jnp.where(core == 0, y, x) for x, y in zip(a, b)]
            tiles += merged(left, right)
        blocks.append(tiles)
    return blocks


def depth_step(kcheb, first, final, *refs):
    core = lax.axis_index("sub")
    block = lax.axis_index("lat") * 2 + core
    blocks = 2 * lax.axis_size("lat")
    terms = refs[-1]
    coefficient, refs = refs[0], refs[1:-1]
    tiles = coefficient.shape[1]
    own = 2 * ROWS
    up_ok = block > 0
    down_ok = block < blocks - 1
    if first:
        parts, refs = whole_blocks(refs[:6]), refs[6:]
    else:
        parts, refs = [[r[i] for i in range(PARTS * tiles)] for r in refs[:3]], refs[3:]
    for i in range(PARTS * tiles):
        mine, a, b = [part[i] for part in parts]
        terms[0, i, pl.ds(own, ROWS), :] = mine
        terms[0, i, pl.ds(own - ROWS, ROWS), :] = jnp.where(up_ok, jnp.where(core == 0, b, a), 0.0)
        terms[0, i, pl.ds(own + ROWS, ROWS), :] = jnp.where(down_ok, jnp.where(core == 0, a, b), 0.0)
    shape = (ROWS, LANES)
    up_scale = jnp.where(up_ok, jnp.full(shape, 0.25, jnp.float32), 0.0)
    down_scale = jnp.where(down_ok, jnp.full(shape, 0.25, jnp.float32), 0.0)
    chebyshev(terms, tiles, kcheb, up_scale, down_scale)
    result = [combined(terms, coefficient, j, tiles, kcheb) for j in range(tiles)]
    images = [sr * rr + si * ri for sr, si, rr, ri in result]
    if not final:
        new_ref, image_ref = refs
        for j in range(tiles):
            for p in range(PARTS):
                new_ref[p * tiles + j] = result[j][p]
            image_ref[j] = images[j]
        return
    fields_ref, here_ref, sub_ref, cross_ref = refs[1:]
    mine, theirs = halves(images, core)
    here_ref[0] = mine
    cross_ref[0] = theirs
    sub_ref[PARTS] = theirs
    for p in range(PARTS):
        fields_ref[p], sub_ref[p] = halves([total[p] for total in result], core)


def early_images(*refs):
    past, (kept_ref, sub_ref, here_ref, cross_ref) = refs[:-5], refs[-4:]
    core = lax.axis_index("sub")
    owners = lax.axis_size("freq")
    here = lax.axis_index("freq")
    each = kept_ref.shape[0]
    empty = jnp.zeros(kept_ref.shape[1:], jnp.float32)
    for depth in range(len(past) + 1):
        if depth < len(past):
            mine, theirs = halves([past[depth][j] for j in range(past[depth].shape[0])], core)
        else:
            mine = theirs = empty
        shift = lax.rem(depth // each - here + owners, owners)
        slot = depth % each

        @pl.when(shift == 0)
        def _():
            kept_ref[slot] = mine
            sub_ref[slot] = theirs

        @pl.when(shift != 0)
        def _():
            here_ref[shift - 1, slot] = mine
            cross_ref[shift - 1, slot] = theirs


def both_rows():
    core = lax.axis_index("sub")
    return [pl.ds(pl.multiple_of(c * ROWS, ROWS), ROWS) for c in (core, 1 - core)]


def assemble_fields(kept_ref, sub_ref, fields_ref):
    mine, theirs = both_rows()
    for p in range(PARTS):
        fields_ref[0, p, mine, :] = kept_ref[p]
        fields_ref[0, p, theirs, :] = sub_ref[p]


def assemble_images(count, *refs):
    early, late, image_ref = refs[: 2 * count], refs[2 * count : 4 * count], refs[-1]
    each = image_ref.shape[0]
    holds_last = lax.axis_index("freq") == lax.axis_size("freq") - 1
    for side, rows in enumerate(both_rows()):
        for d in range(each):
            value = functools.reduce(jnp.add, [r[d] for r in early[side::2]])
            if d == each - 1:
                last = functools.reduce(jnp.add, [r[r.shape[0] - 1] for r in late[side::2]])
                value = value + jnp.where(holds_last, last, 0.0)
            image_ref[d, rows, :] = value


def body(wavefields, velocity, filter_table, freq_pick, slab_order):
    f32 = jnp.float32
    lat = lax.axis_size("lat")
    freq = lax.axis_size("freq")
    bins, _, terms, _ = filter_table.shape
    kcheb = terms - 1
    _, parts, rows, cols = wavefields.shape
    depths = slab_order.shape[0]
    tiles = 2 * cols // LANES
    each = depths // freq
    assert rows == 2 * ROWS and kcheb == ROWS and parts == PARTS and lax.axis_size("sub") == 2

    def call(kernel, outs, args, params=SMALL, specs=None, scratch=(), flops=1 << 20):
        return pl.pallas_call(
            kernel,
            out_shape=tuple(jax.ShapeDtypeStruct(o, f32) for o in outs),
            in_specs=vmem(len(args)) if specs is None else specs,
            out_specs=tuple(vmem(len(outs))),
            scratch_shapes=scratch,
            compiler_params=params,
            cost_estimate=cost(flops),
        )(*args)

    def shifted(value, s):
        return lax.ppermute(value, "freq", [(i, (i + s) % freq) for i in range(freq)])

    def crossed(value, s):
        pairs = [(2 * i + c, 2 * ((i + s) % freq) + 1 - c) for i in range(freq) for c in range(2)]
        return lax.ppermute(value, ("freq", "sub"), pairs)

    slabs = [velocity]
    for s in range(1, freq):
        slabs.append(lax.ppermute(velocity, "freq", [((i + s) % freq, i) for i in range(freq)]))

    table = lax.dynamic_index_in_dim(filter_table, freq_pick[0], 1, keepdims=False)
    table = table.reshape(bins, 2 * terms).T
    table = jnp.pad(table, ((0, 0), (0, LANES - bins)))
    order = jnp.broadcast_to(slab_order[:, None, None], (depths, ROWS, LANES))

    chain = chain_permutation(lat, freq)
    axes = ("lat", "freq", "sub")
    compact = (PARTS * tiles // 2, ROWS, LANES)
    own, mate = call(arrange_fields, (compact, compact), (wavefields,))
    across = lax.ppermute(mate, "sub", SWAP)
    start = (own, across, mate, lax.ppermute(own, "sub", SWAP))
    start += (lax.ppermute(across, axes, chain), lax.ppermute(own, axes, chain))

    strip = (depths, ROWS, cols)
    keep, send = call(pack_velocity, (strip, strip), (order, *slabs))
    theirs = lax.ppermute(send, "sub", SWAP)

    def coefficients_of(depth, after):
        return call(
            functools.partial(coefficients, depth, bins),
            ((2 * terms, tiles, ROWS, LANES),),
            (table, keep, theirs) + after,
        )[0]

    scratch = [pltpu.VMEM((terms, PARTS * tiles, 5 * ROWS, LANES), f32)]
    coefficient = coefficients_of(0, ())
    block = (PARTS * tiles, ROWS, LANES)
    state = start
    images = []
    for depth in range(depths - 1):
        own, image = call(
            functools.partial(depth_step, kcheb, depth == 0, False),
            (block, (tiles, ROWS, LANES)),
            (coefficient, *state),
            params=STEP,
            scratch=scratch,
        )
        images.append(image)
        zmate = lax.ppermute(own, axes, chain)
        state = (own, lax.ppermute(own, "sub", SWAP), zmate)
        coefficient = coefficients_of(depth + 1, (own,))

    row = (each, ROWS, cols)
    outs = (row, row, (freq - 1,) + row, (freq - 1,) + row)
    kept, sub_send, here_send, cross_send = call(early_images, outs, (*images, coefficient))
    early = [kept, lax.ppermute(sub_send, "sub", SWAP)]
    for s in range(1, freq):
        early.append(shifted(here_send[s - 1], s))
        early.append(crossed(cross_send[s - 1], s))

    strip = (ROWS, cols)
    fields, here, sub_send, cross = call(
        functools.partial(depth_step, kcheb, depths == 1, True),
        ((PARTS,) + strip, (1,) + strip, (PARTS + 1,) + strip, (1,) + strip),
        (coefficient, *state, kept),
        params=STEP,
        scratch=scratch,
    )
    sub_got = lax.ppermute(sub_send, "sub", SWAP)
    late = [here, sub_got]
    for s in range(1, freq):
        late += [shifted(here, s), crossed(cross, s)]
    fields = call(assemble_fields, (wavefields.shape,), (fields, sub_got))[0]
    image = call(functools.partial(assemble_images, freq), ((each, rows, cols),), (*early, *late))[0]
    return fields, image


def solution(mesh):
    return jax.shard_map(
        body,
        mesh=mesh,
        in_specs=(
            P(("shots", "freq"), None, "lat", "sub"),
            P("freq", "lat", "sub"),
            P(),
            P("freq"),
            P(),
        ),
        out_specs=(P(("shots", "freq"), None, "lat", "sub"), P(("shots", "freq"), "lat", "sub")),
        check_vma=False,
    )
```

```python
import functools

import jax
import jax.numpy as jnp
from jax import lax
from jax.experimental import pallas as pl
from jax.experimental.pallas import tpu as pltpu
from jax.sharding import PartitionSpec as P


PARTS = 4
LANES = 128
ROWS = 8


def lane_ids():
    return lax.broadcasted_iota(jnp.int32, (ROWS, LANES), 1)


def pick(tile, index):
    return jnp.take_along_axis(tile, index, axis=1)


def straightened(tiles):
    count = len(tiles)
    lane = lane_ids()
    home = lane % count
    natural = []
    for t in range(count):
        index = (LANES // count) * t + lane // count
        out = pick(tiles[0], index)
        for j in range(1, count):
            out = jnp.where(home == j, pick(tiles[j], index), out)
        natural.append(out)
    return natural


def chain_permutation(shots, lat, freq):
    def flat(s, z, f, c):
        return ((s * lat + z) * freq + f) * 2 + c

    pairs = []
    for s in range(shots):
        for f in range(freq):
            for z in range(lat - 1):
                pairs.append((flat(s, z, f, 1), flat(s, z + 1, f, 0)))
                pairs.append((flat(s, z + 1, f, 0), flat(s, z, f, 1)))
            if shots % 2 == 0:
                pairs.append((flat(s, 0, f, 0), flat(s ^ 1, 0, f, 0)))
                pairs.append((flat(s, lat - 1, f, 1), flat(s ^ 1, lat - 1, f, 1)))
    return pairs


SWAP = [(0, 1), (1, 0)]
SMALL = pltpu.CompilerParams(vmem_limit_bytes=4 << 20)
STEP = pltpu.CompilerParams(vmem_limit_bytes=12 << 20)


def vmem(count):
    return [pl.BlockSpec(memory_space=pltpu.VMEM)] * count


def cost(flops):
    return pl.CostEstimate(flops=flops, bytes_accessed=1 << 16, transcendentals=0)


def spread_half(natural, core, out, tiles):
    lane = lane_ids()
    span = LANES // tiles
    home = lane // span - core * (tiles // 2)
    result = []
    for j in range(tiles):
        index = tiles * (lane % span) + j
        value = out[j]
        for t, tile in enumerate(natural):
            got = pick(tile, index)
            value = got if value is None else jnp.where(home == t, got, value)
        result.append(value)
    return result


def compacted(natural):
    half = len(natural)
    lane = lane_ids()
    within = lane % (LANES // 2)
    span = LANES // (2 * half)
    home = within // span
    tiles = []
    for i in range(half):
        index = 2 * half * (within % span) + i + half * (lane // (LANES // 2))
        value = pick(natural[0], index)
        for t in range(1, half):
            value = jnp.where(home == t, pick(natural[t], index), value)
        tiles.append(value)
    return tiles


def merged(left, right):
    middle = LANES // 2
    low = lane_ids() < middle
    first = [jnp.where(low, a, pltpu.roll(b, middle, 1)) for a, b in zip(left, right)]
    second = [jnp.where(low, pltpu.roll(a, middle, 1), b) for a, b in zip(left, right)]
    return first + second


def arrange_fields(x_ref, own_ref, mate_ref):
    half = x_ref.shape[3] // LANES
    for target, rows in zip((own_ref, mate_ref), both_rows()):
        for p in range(PARTS):
            natural = [x_ref[0, p, rows, t * LANES : (t + 1) * LANES] for t in range(half)]
            for i, tile in enumerate(compacted(natural)):
                target[p * half + i] = tile


def pack_velocity(order_ref, *refs):
    slabs, (keep_ref, send_ref) = refs[:-2], refs[-2:]
    core = lax.axis_index("sub")
    here = lax.axis_index("freq")
    count = len(slabs)
    size = slabs[0].shape[0]
    half = keep_ref.shape[2] // LANES
    for target, row in ((keep_ref, core), (send_ref, 1 - core)):
        rows = pl.ds(pl.multiple_of(row * ROWS, ROWS), ROWS)
        for t in range(half):
            columns = slice(t * LANES, (t + 1) * LANES)
            values = [[slabs[s][i, rows, columns] for i in range(size)] for s in range(count)]
            for d in range(keep_ref.shape[0]):
                stored = order_ref[d]
                value = values[0][0]
                for s in range(count):
                    first = lax.rem(here + s, count) * size
                    for i in range(size):
                        if s or i:
                            value = jnp.where(stored == first + i, values[s][i], value)
                target[d, :, columns] = value


def chebyshev(terms, tiles, kcheb, up_scale, down_scale):
    lane = lane_ids()
    sub = lax.broadcasted_iota(jnp.int32, (ROWS, LANES), 0)
    first = lane == 0
    last = lane == LANES - 1
    half = ROWS // 2
    inside = jnp.full((ROWS, LANES), 0.25, jnp.float32)
    upper = jnp.where(sub < half, up_scale, inside)
    lower = jnp.where(sub >= half, down_scale, inside)
    own = 2 * ROWS
    for k in range(kcheb):
        reach = kcheb - (k + 1)
        if reach > half:
            windows = ((own - ROWS, up_scale), (own, inside), (own + ROWS, down_scale))
        elif reach > 0:
            windows = ((own - half, upper), (own + half, lower))
        else:
            windows = ((own, inside),)
        for row, scale in windows:
            for p in range(PARTS):
                base = p * tiles
                twice = []
                sums = []
                for j in range(tiles):
                    value = terms[k, base + j, pl.ds(row, ROWS), :]
                    double = value + value
                    around = terms[k, base + j, pl.ds(row - 1, ROWS), :] + terms[k, base + j, pl.ds(row + 1, ROWS), :]
                    sums.append(around + double)
                    twice.append(value if k == 0 else double)
                before = jnp.where(first, 0.0, pltpu.roll(sums[tiles - 1], 1, 1))
                after = jnp.where(last, 0.0, pltpu.roll(sums[0], LANES - 1, 1))
                pair = [sums[j] + sums[j + 1] for j in range(tiles - 1)]
                full = [pair[0] + (sums[0] + before)]
                full += [pair[j - 1] + pair[j] for j in range(1, tiles - 1)]
                full.append(pair[tiles - 2] + (sums[tiles - 1] + after))
                for j in range(tiles):
                    if k == 0:
                        new = (0.5 * scale) * full[j] - twice[j]
                    else:
                        new = scale * full[j] - (twice[j] + terms[k - 1, base + j, pl.ds(row, ROWS), :])
                    terms[k + 1, base + j, pl.ds(row, ROWS), :] = new


def bins_of(depth, bins, keep_ref, other_ref, tiles):
    core = lax.axis_index("sub")
    half = tiles // 2
    velocity = [None] * tiles
    for ref, home in ((keep_ref, core), (other_ref, 1 - core)):
        strips = [ref[depth, :, t * LANES : (t + 1) * LANES] for t in range(half)]
        velocity = spread_half(strips, home, velocity, tiles)
    lows = [jnp.clip(v.astype(jnp.int32), 0, bins - 1) for v in velocity]
    return lows, [v - low.astype(jnp.float32) for v, low in zip(velocity, lows)]


def coefficients(depth, bins, table_ref, keep_ref, other_ref, *refs):
    out_ref = refs[-1]
    count, tiles = out_ref.shape[:2]
    lows, parts = bins_of(depth, bins, keep_ref, other_ref, tiles)
    table = table_ref[...]
    step = pltpu.roll(table, LANES - 1, 1) - table
    for i in range(count):
        at_low = jnp.broadcast_to(table[i : i + 1], (ROWS, LANES))
        rise = jnp.broadcast_to(step[i : i + 1], (ROWS, LANES))
        for j in range(tiles):
            out_ref[i, j] = pick(at_low, lows[j]) + parts[j] * pick(rise, lows[j])


def combined(terms, coefficient, j, tiles, kcheb):
    own = 2 * ROWS
    total = None
    for k in range(kcheb + 1):
        a = coefficient(2 * k, j)
        b = coefficient(2 * k + 1, j)
        sr, si, rr, ri = [terms[k, p * tiles + j, pl.ds(own, ROWS), :] for p in range(PARTS)]
        adds = (a * sr + b * si, a * si - b * sr, a * rr - b * ri, a * ri + b * rr)
        total = adds if total is None else tuple(y + x for x, y in zip(adds, total))
    return total


def halves(stack, core):
    natural = straightened(stack)
    half = len(natural) // 2
    left, right = natural[:half], natural[half:]
    mine = [jnp.where(core == 0, a, b) for a, b in zip(left, right)]
    theirs = [jnp.where(core == 0, b, a) for a, b in zip(left, right)]
    return jnp.concatenate(mine, axis=1), jnp.concatenate(theirs, axis=1)


def whole_blocks(refs):
    core = lax.axis_index("sub")
    half = refs[0].shape[0] // PARTS
    blocks = []
    for ours, others in (refs[0:2], refs[2:4], refs[4:6]):
        tiles = []
        for p in range(PARTS):
            a = [ours[p * half + i] for i in range(half)]
            b = [others[p * half + i] for i in range(half)]
            left = [jnp.where(core == 0, x, y) for x, y in zip(a, b)]
            right = [jnp.where(core == 0, y, x) for x, y in zip(a, b)]
            tiles += merged(left, right)
        blocks.append(tiles)
    return blocks


def depth_step(kcheb, bins, first, final, *refs):
    core = lax.axis_index("sub")
    block = lax.axis_index("lat") * 2 + core
    blocks = 2 * lax.axis_size("lat")
    refs, terms, lookup = refs[:-2], refs[-2], refs[-1]
    tiles = terms.shape[1] // PARTS
    if first:
        (table_ref, keep_ref, other_ref), refs = refs[:3], refs[3:]
        table = table_ref[...]
        step = pltpu.roll(table, LANES - 1, 1) - table
        for i in range(2 * (kcheb + 1)):
            lookup[0, i] = jnp.broadcast_to(table[i : i + 1], (ROWS, LANES))
            lookup[1, i] = jnp.broadcast_to(step[i : i + 1], (ROWS, LANES))
        lows, between = bins_of(0, bins, keep_ref, other_ref, tiles)

        def coefficient(i, j):
            return pick(lookup[0, i], lows[j]) + between[j] * pick(lookup[1, i], lows[j])
    else:
        ready, refs = refs[0], refs[1:]

        def coefficient(i, j):
            return ready[i, j]

    own = 2 * ROWS
    up_ok = block > 0
    down_ok = block < blocks - 1
    if first:
        parts, refs = whole_blocks(refs[:6]), refs[6:]
    else:
        parts, refs = [[r[i] for i in range(PARTS * tiles)] for r in refs[:3]], refs[3:]
    for i in range(PARTS * tiles):
        mine, a, b = [part[i] for part in parts]
        terms[0, i, pl.ds(own, ROWS), :] = mine
        terms[0, i, pl.ds(own - ROWS, ROWS), :] = jnp.where(up_ok, jnp.where(core == 0, b, a), 0.0)
        terms[0, i, pl.ds(own + ROWS, ROWS), :] = jnp.where(down_ok, jnp.where(core == 0, a, b), 0.0)
    shape = (ROWS, LANES)
    up_scale = jnp.where(up_ok, jnp.full(shape, 0.25, jnp.float32), 0.0)
    down_scale = jnp.where(down_ok, jnp.full(shape, 0.25, jnp.float32), 0.0)
    chebyshev(terms, tiles, kcheb, up_scale, down_scale)
    result = [combined(terms, coefficient, j, tiles, kcheb) for j in range(tiles)]
    images = [sr * rr + si * ri for sr, si, rr, ri in result]
    if not final:
        new_ref, image_ref = refs
        for j in range(tiles):
            for p in range(PARTS):
                new_ref[p * tiles + j] = result[j][p]
            image_ref[j] = images[j]
        return
    fields_ref, here_ref, sub_ref, cross_ref = refs[1:]
    mine, theirs = halves(images, core)
    here_ref[0] = mine
    cross_ref[0] = theirs
    sub_ref[PARTS] = theirs
    for p in range(PARTS):
        fields_ref[p], sub_ref[p] = halves([total[p] for total in result], core)


def early_images(*refs):
    past, (kept_ref, sub_ref, here_ref, cross_ref) = refs[:-5], refs[-4:]
    core = lax.axis_index("sub")
    owners = lax.axis_size("freq")
    here = lax.axis_index("freq")
    each = kept_ref.shape[0]
    empty = jnp.zeros(kept_ref.shape[1:], jnp.float32)
    for depth in range(len(past) + 1):
        if depth < len(past):
            mine, theirs = halves([past[depth][j] for j in range(past[depth].shape[0])], core)
        else:
            mine = theirs = empty
        shift = lax.rem(depth // each - here + owners, owners)
        slot = depth % each

        @pl.when(shift == 0)
        def _():
            kept_ref[slot] = mine
            sub_ref[slot] = theirs

        @pl.when(shift != 0)
        def _():
            here_ref[shift - 1, slot] = mine
            cross_ref[shift - 1, slot] = theirs


def both_rows():
    core = lax.axis_index("sub")
    return [pl.ds(pl.multiple_of(c * ROWS, ROWS), ROWS) for c in (core, 1 - core)]


def assemble_fields(kept_ref, sub_ref, fields_ref):
    mine, theirs = both_rows()
    for p in range(PARTS):
        fields_ref[0, p, mine, :] = kept_ref[p]
        fields_ref[0, p, theirs, :] = sub_ref[p]


def assemble_images(count, *refs):
    early, late, image_ref = refs[: 2 * count], refs[2 * count : 4 * count], refs[-1]
    each = image_ref.shape[0]
    holds_last = lax.axis_index("freq") == lax.axis_size("freq") - 1
    for side, rows in enumerate(both_rows()):
        for d in range(each):
            value = functools.reduce(jnp.add, [r[d] for r in early[side::2]])
            if d == each - 1:
                last = functools.reduce(jnp.add, [r[r.shape[0] - 1] for r in late[side::2]])
                value = value + jnp.where(holds_last, last, 0.0)
            image_ref[d, rows, :] = value


def body(wavefields, velocity, filter_table, freq_pick, slab_order):
    f32 = jnp.float32
    lat = lax.axis_size("lat")
    freq = lax.axis_size("freq")
    bins, _, terms, _ = filter_table.shape
    kcheb = terms - 1
    _, parts, rows, cols = wavefields.shape
    depths = slab_order.shape[0]
    tiles = 2 * cols // LANES
    each = depths // freq
    assert rows == 2 * ROWS and kcheb == ROWS and parts == PARTS and lax.axis_size("sub") == 2

    def call(kernel, outs, args, params=SMALL, specs=None, scratch=(), flops=1 << 20):
        return pl.pallas_call(
            kernel,
            out_shape=tuple(jax.ShapeDtypeStruct(o, f32) for o in outs),
            in_specs=vmem(len(args)) if specs is None else specs,
            out_specs=tuple(vmem(len(outs))),
            scratch_shapes=scratch,
            compiler_params=params,
            cost_estimate=cost(flops),
        )(*args)

    def shifted(value, s):
        return lax.ppermute(value, "freq", [(i, (i + s) % freq) for i in range(freq)])

    def crossed(value, s):
        pairs = [(2 * i + c, 2 * ((i + s) % freq) + 1 - c) for i in range(freq) for c in range(2)]
        return lax.ppermute(value, ("freq", "sub"), pairs)

    slabs = [velocity]
    for s in range(1, freq):
        slabs.append(lax.ppermute(velocity, "freq", [((i + s) % freq, i) for i in range(freq)]))

    table = lax.dynamic_index_in_dim(filter_table, freq_pick[0], 1, keepdims=False)
    table = table.reshape(bins, 2 * terms).T
    table = jnp.pad(table, ((0, 0), (0, LANES - bins)))
    order = jnp.broadcast_to(slab_order[:, None, None], (depths, ROWS, LANES))

    chain = chain_permutation(lax.axis_size("shots"), lat, freq)
    axes = ("shots", "lat", "freq", "sub")
    compact = (PARTS * tiles // 2, ROWS, LANES)
    own, mate = call(arrange_fields, (compact, compact), (wavefields,))
    across = lax.ppermute(mate, "sub", SWAP)
    start = (own, across, mate, lax.ppermute(own, "sub", SWAP))
    start += (lax.ppermute(across, axes, chain), lax.ppermute(own, axes, chain))

    strip = (depths, ROWS, cols)
    keep, send = call(pack_velocity, (strip, strip), (order, *slabs))
    theirs = lax.ppermute(send, "sub", SWAP)

    def coefficients_of(depth, after):
        return call(
            functools.partial(coefficients, depth, bins),
            ((2 * terms, tiles, ROWS, LANES),),
            (table, keep, theirs) + after,
        )[0]

    scratch = [
        pltpu.VMEM((terms, PARTS * tiles, 5 * ROWS, LANES), f32),
        pltpu.VMEM((2, 2 * terms, ROWS, LANES), f32),
    ]
    ready = [(table, keep, theirs)] + [None] * (depths - 1)
    block = (PARTS * tiles, ROWS, LANES)
    state = start
    images = []
    for depth in range(depths - 1):
        own, image = call(
            functools.partial(depth_step, kcheb, bins, depth == 0, False),
            (block, (tiles, ROWS, LANES)),
            (*ready[depth], *state),
            params=STEP,
            scratch=scratch,
        )
        images.append(image)
        zmate = lax.ppermute(own, axes, chain)
        state = (own, lax.ppermute(own, "sub", SWAP), zmate)
        wanted = [depth + 1] if depth + 1 < depths - 1 else []
        if depth == max(depths - 3, 0):
            wanted.append(depths - 1)
        for d in wanted:
            ready[d] = (coefficients_of(d, (own,)),)

    row = (each, ROWS, cols)
    outs = (row, row, (freq - 1,) + row, (freq - 1,) + row)
    kept, sub_send, here_send, cross_send = call(early_images, outs, (*images, *ready[-1]))
    early = [kept, lax.ppermute(sub_send, "sub", SWAP)]
    for s in range(1, freq):
        early.append(shifted(here_send[s - 1], s))
        early.append(crossed(cross_send[s - 1], s))

    strip = (ROWS, cols)
    fields, here, sub_send, cross = call(
        functools.partial(depth_step, kcheb, bins, depths == 1, True),
        ((PARTS,) + strip, (1,) + strip, (PARTS + 1,) + strip, (1,) + strip),
        (*ready[-1], *state, kept),
        params=STEP,
        scratch=scratch,
    )
    sub_got = lax.ppermute(sub_send, "sub", SWAP)
    late = [here, sub_got]
    for s in range(1, freq):
        late.append(shifted(here, s))
        late.append(crossed(cross, s))
    fields = call(assemble_fields, (wavefields.shape,), (fields, sub_got))[0]
    image = call(functools.partial(assemble_images, freq), ((each, rows, cols),), (*early, *late))[0]
    return fields, image


def solution(mesh):
    return jax.shard_map(
        body,
        mesh=mesh,
        in_specs=(
            P(("shots", "freq"), None, "lat", "sub"),
            P("freq", "lat", "sub"),
            P(),
            P("freq"),
            P(),
        ),
        out_specs=(P(("shots", "freq"), None, "lat", "sub"), P(("shots", "freq"), "lat", "sub")),
        check_vma=False,
    )
```

```python
import functools

import jax
import jax.numpy as jnp
from jax import lax
from jax.experimental import pallas as pl
from jax.experimental.pallas import tpu as pltpu
from jax.sharding import PartitionSpec as P


PARTS = 4
LANES = 128
ROWS = 8


def lane_ids():
    return lax.broadcasted_iota(jnp.int32, (ROWS, LANES), 1)


def pick(tile, index):
    return jnp.take_along_axis(tile, index, axis=1)


def straightened(tiles):
    count = len(tiles)
    lane = lane_ids()
    home = lane % count
    natural = []
    for t in range(count):
        index = (LANES // count) * t + lane // count
        out = pick(tiles[0], index)
        for j in range(1, count):
            out = jnp.where(home == j, pick(tiles[j], index), out)
        natural.append(out)
    return natural


def chain_permutation(shots, lat, freq):
    def flat(s, z, f, c):
        return ((s * lat + z) * freq + f) * 2 + c

    pairs = []
    for s in range(shots):
        for f in range(freq):
            for z in range(lat - 1):
                pairs.append((flat(s, z, f, 1), flat(s, z + 1, f, 0)))
                pairs.append((flat(s, z + 1, f, 0), flat(s, z, f, 1)))
            if shots % 2 == 0:
                pairs.append((flat(s, 0, f, 0), flat(s ^ 1, 0, f, 0)))
                pairs.append((flat(s, lat - 1, f, 1), flat(s ^ 1, lat - 1, f, 1)))
    return pairs


SWAP = [(0, 1), (1, 0)]
SMALL = pltpu.CompilerParams(vmem_limit_bytes=4 << 20)
STEP = pltpu.CompilerParams(vmem_limit_bytes=12 << 20)


def vmem(count):
    return [pl.BlockSpec(memory_space=pltpu.VMEM)] * count


def cost(flops):
    return pl.CostEstimate(flops=flops, bytes_accessed=1 << 16, transcendentals=0)


def spread_half(natural, core, out, tiles):
    lane = lane_ids()
    span = LANES // tiles
    home = lane // span - core * (tiles // 2)
    result = []
    for j in range(tiles):
        index = tiles * (lane % span) + j
        value = out[j]
        for t, tile in enumerate(natural):
            got = pick(tile, index)
            value = got if value is None else jnp.where(home == t, got, value)
        result.append(value)
    return result


def compacted(natural):
    half = len(natural)
    lane = lane_ids()
    within = lane % (LANES // 2)
    span = LANES // (2 * half)
    home = within // span
    tiles = []
    for i in range(half):
        index = 2 * half * (within % span) + i + half * (lane // (LANES // 2))
        value = pick(natural[0], index)
        for t in range(1, half):
            value = jnp.where(home == t, pick(natural[t], index), value)
        tiles.append(value)
    return tiles


def merged(left, right):
    middle = LANES // 2
    low = lane_ids() < middle
    first = [jnp.where(low, a, pltpu.roll(b, middle, 1)) for a, b in zip(left, right)]
    second = [jnp.where(low, pltpu.roll(a, middle, 1), b) for a, b in zip(left, right)]
    return first + second


def arrange_fields(x_ref, own_ref, mate_ref):
    half = x_ref.shape[3] // LANES
    for target, rows in zip((own_ref, mate_ref), both_rows()):
        for p in range(PARTS):
            natural = [x_ref[0, p, rows, t * LANES : (t + 1) * LANES] for t in range(half)]
            for i, tile in enumerate(compacted(natural)):
                target[p * half + i] = tile


def pack_block(mate, part_ref, other_ref, *refs):
    core = lax.axis_index("sub")
    block_ref = refs[-1]
    half = part_ref.shape[0] // PARTS
    rows = both_rows()[1 if mate else 0]
    for p in range(PARTS):
        mine = [part_ref[p * half + i] for i in range(half)]
        theirs = compacted([other_ref[0, p, rows, t * LANES : (t + 1) * LANES] for t in range(half)])
        left = [jnp.where(core == 0, x, y) for x, y in zip(mine, theirs)]
        right = [jnp.where(core == 0, y, x) for x, y in zip(mine, theirs)]
        for j, tile in enumerate(merged(left, right)):
            block_ref[2 * p * half + j] = tile


def pack_velocity(order_ref, *refs):
    slabs, (keep_ref, send_ref) = refs[:-2], refs[-2:]
    core = lax.axis_index("sub")
    here = lax.axis_index("freq")
    count = len(slabs)
    size = slabs[0].shape[0]
    half = keep_ref.shape[2] // LANES
    for target, row in ((keep_ref, core), (send_ref, 1 - core)):
        rows = pl.ds(pl.multiple_of(row * ROWS, ROWS), ROWS)
        for t in range(half):
            columns = slice(t * LANES, (t + 1) * LANES)
            values = [[slabs[s][i, rows, columns] for i in range(size)] for s in range(count)]
            for d in range(keep_ref.shape[0]):
                stored = order_ref[d]
                value = values[0][0]
                for s in range(count):
                    first = lax.rem(here + s, count) * size
                    for i in range(size):
                        if s or i:
                            value = jnp.where(stored == first + i, values[s][i], value)
                target[d, :, columns] = value


def chebyshev(terms, tiles, kcheb, up_scale, down_scale):
    lane = lane_ids()
    sub = lax.broadcasted_iota(jnp.int32, (ROWS, LANES), 0)
    first = lane == 0
    last = lane == LANES - 1
    half = ROWS // 2
    inside = jnp.full((ROWS, LANES), 0.25, jnp.float32)
    upper = jnp.where(sub < half, up_scale, inside)
    lower = jnp.where(sub >= half, down_scale, inside)
    own = 2 * ROWS
    for k in range(kcheb):
        reach = kcheb - (k + 1)
        if reach > half:
            windows = ((own - ROWS, up_scale), (own, inside), (own + ROWS, down_scale))
        elif reach > 0:
            windows = ((own - half, upper), (own + half, lower))
        else:
            windows = ((own, inside),)
        for row, scale in windows:
            for p in range(PARTS):
                base = p * tiles
                twice = []
                sums = []
                for j in range(tiles):
                    value = terms[k, base + j, pl.ds(row, ROWS), :]
                    double = value + value
                    around = terms[k, base + j, pl.ds(row - 1, ROWS), :] + terms[k, base + j, pl.ds(row + 1, ROWS), :]
                    sums.append(around + double)
                    twice.append(value if k == 0 else double)
                before = jnp.where(first, 0.0, pltpu.roll(sums[tiles - 1], 1, 1))
                after = jnp.where(last, 0.0, pltpu.roll(sums[0], LANES - 1, 1))
                pair = [sums[j] + sums[j + 1] for j in range(tiles - 1)]
                full = [pair[0] + (sums[0] + before)]
                full += [pair[j - 1] + pair[j] for j in range(1, tiles - 1)]
                full.append(pair[tiles - 2] + (sums[tiles - 1] + after))
                for j in range(tiles):
                    if k == 0:
                        new = (0.5 * scale) * full[j] - twice[j]
                    else:
                        new = scale * full[j] - (twice[j] + terms[k - 1, base + j, pl.ds(row, ROWS), :])
                    terms[k + 1, base + j, pl.ds(row, ROWS), :] = new


def bins_of(depth, bins, keep_ref, other_ref, tiles):
    core = lax.axis_index("sub")
    half = tiles // 2
    velocity = [None] * tiles
    for ref, home in ((keep_ref, core), (other_ref, 1 - core)):
        strips = [ref[depth, :, t * LANES : (t + 1) * LANES] for t in range(half)]
        velocity = spread_half(strips, home, velocity, tiles)
    lows = [jnp.clip(v.astype(jnp.int32), 0, bins - 1) for v in velocity]
    return lows, [v - low.astype(jnp.float32) for v, low in zip(velocity, lows)]


def coefficients(depth, bins, table_ref, keep_ref, other_ref, *refs):
    out_ref = refs[-1]
    count, tiles = out_ref.shape[:2]
    lows, parts = bins_of(depth, bins, keep_ref, other_ref, tiles)
    table = table_ref[...]
    step = pltpu.roll(table, LANES - 1, 1) - table
    for i in range(count):
        at_low = jnp.broadcast_to(table[i : i + 1], (ROWS, LANES))
        rise = jnp.broadcast_to(step[i : i + 1], (ROWS, LANES))
        for j in range(tiles):
            out_ref[i, j] = pick(at_low, lows[j]) + parts[j] * pick(rise, lows[j])


def combined(terms, coefficient, j, tiles, kcheb):
    own = 2 * ROWS
    total = None
    for k in range(kcheb + 1):
        a = coefficient(2 * k, j)
        b = coefficient(2 * k + 1, j)
        sr, si, rr, ri = [terms[k, p * tiles + j, pl.ds(own, ROWS), :] for p in range(PARTS)]
        adds = (a * sr + b * si, a * si - b * sr, a * rr - b * ri, a * ri + b * rr)
        total = adds if total is None else tuple(y + x for x, y in zip(adds, total))
    return total


def halves(stack, core):
    natural = straightened(stack)
    half = len(natural) // 2
    left, right = natural[:half], natural[half:]
    mine = [jnp.where(core == 0, a, b) for a, b in zip(left, right)]
    theirs = [jnp.where(core == 0, b, a) for a, b in zip(left, right)]
    return jnp.concatenate(mine, axis=1), jnp.concatenate(theirs, axis=1)


def depth_step(kcheb, bins, first, final, *refs):
    core = lax.axis_index("sub")
    block = lax.axis_index("lat") * 2 + core
    blocks = 2 * lax.axis_size("lat")
    refs, terms, lookup = refs[:-2], refs[-2], refs[-1]
    tiles = terms.shape[1] // PARTS
    if first:
        (table_ref, keep_ref, other_ref), refs = refs[:3], refs[3:]
        table = table_ref[...]
        step = pltpu.roll(table, LANES - 1, 1) - table
        for i in range(2 * (kcheb + 1)):
            lookup[0, i] = jnp.broadcast_to(table[i : i + 1], (ROWS, LANES))
            lookup[1, i] = jnp.broadcast_to(step[i : i + 1], (ROWS, LANES))
        lows, between = bins_of(0, bins, keep_ref, other_ref, tiles)

        def coefficient(i, j):
            return pick(lookup[0, i], lows[j]) + between[j] * pick(lookup[1, i], lows[j])
    else:
        ready, refs = refs[0], refs[1:]

        def coefficient(i, j):
            return ready[i, j]

    own = 2 * ROWS
    up_ok = block > 0
    down_ok = block < blocks - 1
    sources, refs = refs[:3], refs[3:]
    for i in range(PARTS * tiles):
        mine, a, b = [source[i] for source in sources]
        terms[0, i, pl.ds(own, ROWS), :] = mine
        terms[0, i, pl.ds(own - ROWS, ROWS), :] = jnp.where(up_ok, jnp.where(core == 0, b, a), 0.0)
        terms[0, i, pl.ds(own + ROWS, ROWS), :] = jnp.where(down_ok, jnp.where(core == 0, a, b), 0.0)
    shape = (ROWS, LANES)
    up_scale = jnp.where(up_ok, jnp.full(shape, 0.25, jnp.float32), 0.0)
    down_scale = jnp.where(down_ok, jnp.full(shape, 0.25, jnp.float32), 0.0)
    chebyshev(terms, tiles, kcheb, up_scale, down_scale)
    result = [combined(terms, coefficient, j, tiles, kcheb) for j in range(tiles)]
    images = [sr * rr + si * ri for sr, si, rr, ri in result]
    if not final:
        new_ref, image_ref = refs
        for j in range(tiles):
            for p in range(PARTS):
                new_ref[p * tiles + j] = result[j][p]
            image_ref[j] = images[j]
        return
    fields_ref, here_ref, sub_ref, cross_ref = refs[1:]
    mine, theirs = halves(images, core)
    here_ref[0] = mine
    cross_ref[0] = theirs
    sub_ref[PARTS] = theirs
    for p in range(PARTS):
        fields_ref[p], sub_ref[p] = halves([total[p] for total in result], core)


def early_images(*refs):
    past, (kept_ref, sub_ref, here_ref, cross_ref) = refs[:-5], refs[-4:]
    core = lax.axis_index("sub")
    owners = lax.axis_size("freq")
    here = lax.axis_index("freq")
    each = kept_ref.shape[0]
    empty = jnp.zeros(kept_ref.shape[1:], jnp.float32)
    for depth in range(len(past) + 1):
        if depth < len(past):
            mine, theirs = halves([past[depth][j] for j in range(past[depth].shape[0])], core)
        else:
            mine = theirs = empty
        shift = lax.rem(depth // each - here + owners, owners)
        slot = depth % each

        @pl.when(shift == 0)
        def _():
            kept_ref[slot] = mine
            sub_ref[slot] = theirs

        @pl.when(shift != 0)
        def _():
            here_ref[shift - 1, slot] = mine
            cross_ref[shift - 1, slot] = theirs


def both_rows():
    core = lax.axis_index("sub")
    return [pl.ds(pl.multiple_of(c * ROWS, ROWS), ROWS) for c in (core, 1 - core)]


def assemble_fields(kept_ref, sub_ref, fields_ref):
    mine, theirs = both_rows()
    for p in range(PARTS):
        fields_ref[0, p, mine, :] = kept_ref[p]
        fields_ref[0, p, theirs, :] = sub_ref[p]


def assemble_images(count, *refs):
    early, late, image_ref = refs[: 2 * count], refs[2 * count : 4 * count], refs[-1]
    each = image_ref.shape[0]
    holds_last = lax.axis_index("freq") == lax.axis_size("freq") - 1
    for side, rows in enumerate(both_rows()):
        for d in range(each):
            value = functools.reduce(jnp.add, [r[d] for r in early[side::2]])
            if d == each - 1:
                last = functools.reduce(jnp.add, [r[r.shape[0] - 1] for r in late[side::2]])
                value = value + jnp.where(holds_last, last, 0.0)
            image_ref[d, rows, :] = value


def body(wavefields, velocity, filter_table, freq_pick, slab_order):
    f32 = jnp.float32
    lat = lax.axis_size("lat")
    freq = lax.axis_size("freq")
    bins, _, terms, _ = filter_table.shape
    kcheb = terms - 1
    _, parts, rows, cols = wavefields.shape
    depths = slab_order.shape[0]
    tiles = 2 * cols // LANES
    each = depths // freq
    assert rows == 2 * ROWS and kcheb == ROWS and parts == PARTS and lax.axis_size("sub") == 2

    def call(kernel, outs, args, params=SMALL, specs=None, scratch=(), flops=1 << 20):
        return pl.pallas_call(
            kernel,
            out_shape=tuple(jax.ShapeDtypeStruct(o, f32) for o in outs),
            in_specs=vmem(len(args)) if specs is None else specs,
            out_specs=tuple(vmem(len(outs))),
            scratch_shapes=scratch,
            compiler_params=params,
            cost_estimate=cost(flops),
        )(*args)

    def shifted(value, s):
        return lax.ppermute(value, "freq", [(i, (i + s) % freq) for i in range(freq)])

    def crossed(value, s):
        pairs = [(2 * i + c, 2 * ((i + s) % freq) + 1 - c) for i in range(freq) for c in range(2)]
        return lax.ppermute(value, ("freq", "sub"), pairs)

    slabs = [velocity]
    for s in range(1, freq):
        slabs.append(lax.ppermute(velocity, "freq", [((i + s) % freq, i) for i in range(freq)]))

    table = lax.dynamic_index_in_dim(filter_table, freq_pick[0], 1, keepdims=False)
    table = table.reshape(bins, 2 * terms).T
    table = jnp.pad(table, ((0, 0), (0, LANES - bins)))
    order = jnp.broadcast_to(slab_order[:, None, None], (depths, ROWS, LANES))

    chain = chain_permutation(lax.axis_size("shots"), lat, freq)
    axes = ("shots", "lat", "freq", "sub")
    compact = (PARTS * tiles // 2, ROWS, LANES)
    block = (PARTS * tiles, ROWS, LANES)
    other = lax.ppermute(wavefields, "sub", SWAP)
    own_part, mate_part = call(arrange_fields, (compact, compact), (wavefields,))
    own = call(functools.partial(pack_block, False), (block,), (own_part, other))[0]
    zmate = lax.ppermute(own, axes, chain)
    mate = call(functools.partial(pack_block, True), (block,), (mate_part, other, own))[0]

    strip = (depths, ROWS, cols)
    keep, send = call(pack_velocity, (strip, strip), (order, *slabs))
    theirs = lax.ppermute(send, "sub", SWAP)

    def coefficients_of(depth, after):
        return call(
            functools.partial(coefficients, depth, bins),
            ((2 * terms, tiles, ROWS, LANES),),
            (table, keep, theirs) + after,
        )[0]

    scratch = [
        pltpu.VMEM((terms, PARTS * tiles, 5 * ROWS, LANES), f32),
        pltpu.VMEM((2, 2 * terms, ROWS, LANES), f32),
    ]
    ready = [(table, keep, theirs)] + [None] * (depths - 1)
    state = (own, mate, zmate)
    images = []
    for depth in range(depths - 1):
        own, image = call(
            functools.partial(depth_step, kcheb, bins, depth == 0, False),
            (block, (tiles, ROWS, LANES)),
            (*ready[depth], *state),
            params=STEP,
            scratch=scratch,
        )
        images.append(image)
        zmate = lax.ppermute(own, axes, chain)
        mate = lax.ppermute(own, "sub", SWAP)
        state = (own, mate, zmate)
        wanted = [depth + 1] if depth + 1 < depths - 1 else []
        if depth == max(depths - 3, 0):
            wanted.append(depths - 1)
        for d in wanted:
            ready[d] = (coefficients_of(d, (own,)),)

    row = (each, ROWS, cols)
    outs = (row, row, (freq - 1,) + row, (freq - 1,) + row)
    kept, sub_send, here_send, cross_send = call(early_images, outs, (*images, *ready[-1]))
    early = [kept, lax.ppermute(sub_send, "sub", SWAP)]
    for s in range(1, freq):
        early.append(shifted(here_send[s - 1], s))
        early.append(crossed(cross_send[s - 1], s))

    strip = (ROWS, cols)
    fields, here, sub_send, cross = call(
        functools.partial(depth_step, kcheb, bins, depths == 1, True),
        ((PARTS,) + strip, (1,) + strip, (PARTS + 1,) + strip, (1,) + strip),
        (*ready[-1], *state, kept),
        params=STEP,
        scratch=scratch,
    )
    sub_got = lax.ppermute(sub_send, "sub", SWAP)
    late = [here, sub_got]
    for s in range(1, freq):
        late.append(shifted(here, s))
        late.append(crossed(cross, s))
    fields = call(assemble_fields, (wavefields.shape,), (fields, sub_got))[0]
    image = call(functools.partial(assemble_images, freq), ((each, rows, cols),), (*early, *late))[0]
    return fields, image


def solution(mesh):
    return jax.shard_map(
        body,
        mesh=mesh,
        in_specs=(
            P(("shots", "freq"), None, "lat", "sub"),
            P("freq", "lat", "sub"),
            P(),
            P("freq"),
            P(),
        ),
        out_specs=(P(("shots", "freq"), None, "lat", "sub"), P(("shots", "freq"), "lat", "sub")),
        check_vma=False,
    )
```

```python
import functools

import jax
import jax.numpy as jnp
from jax import lax
from jax.experimental import pallas as pl
from jax.experimental.pallas import tpu as pltpu
from jax.sharding import PartitionSpec as P


PARTS = 4
LANES = 128
ROWS = 8


def lane_ids():
    return lax.broadcasted_iota(jnp.int32, (ROWS, LANES), 1)


def pick(tile, index):
    return jnp.take_along_axis(tile, index, axis=1)


def straightened(tiles):
    count = len(tiles)
    lane = lane_ids()
    home = lane % count
    natural = []
    for t in range(count):
        index = (LANES // count) * t + lane // count
        out = pick(tiles[0], index)
        for j in range(1, count):
            out = jnp.where(home == j, pick(tiles[j], index), out)
        natural.append(out)
    return natural


def chain_permutation(shots, lat, freq):
    def flat(s, z, f, c):
        return ((s * lat + z) * freq + f) * 2 + c

    pairs = []
    for s in range(shots):
        for f in range(freq):
            for z in range(lat - 1):
                pairs.append((flat(s, z, f, 1), flat(s, z + 1, f, 0)))
                pairs.append((flat(s, z + 1, f, 0), flat(s, z, f, 1)))
            if shots % 2 == 0:
                pairs.append((flat(s, 0, f, 0), flat(s ^ 1, 0, f, 0)))
                pairs.append((flat(s, lat - 1, f, 1), flat(s ^ 1, lat - 1, f, 1)))
    return pairs


SWAP = [(0, 1), (1, 0)]
SMALL = pltpu.CompilerParams(vmem_limit_bytes=4 << 20)
STEP = pltpu.CompilerParams(vmem_limit_bytes=12 << 20)


def vmem(count):
    return [pl.BlockSpec(memory_space=pltpu.VMEM)] * count


def cost(flops):
    return pl.CostEstimate(flops=flops, bytes_accessed=1 << 16, transcendentals=0)


def spread_half(natural, core, out, tiles):
    lane = lane_ids()
    span = LANES // tiles
    home = lane // span - core * (tiles // 2)
    result = []
    for j in range(tiles):
        index = tiles * (lane % span) + j
        value = out[j]
        for t, tile in enumerate(natural):
            got = pick(tile, index)
            value = got if value is None else jnp.where(home == t, got, value)
        result.append(value)
    return result


def compacted(natural):
    half = len(natural)
    lane = lane_ids()
    within = lane % (LANES // 2)
    span = LANES // (2 * half)
    home = within // span
    tiles = []
    for i in range(half):
        index = 2 * half * (within % span) + i + half * (lane // (LANES // 2))
        value = pick(natural[0], index)
        for t in range(1, half):
            value = jnp.where(home == t, pick(natural[t], index), value)
        tiles.append(value)
    return tiles


def merged(left, right):
    middle = LANES // 2
    low = lane_ids() < middle
    first = [jnp.where(low, a, pltpu.roll(b, middle, 1)) for a, b in zip(left, right)]
    second = [jnp.where(low, pltpu.roll(a, middle, 1), b) for a, b in zip(left, right)]
    return first + second


def parted(tiles, core):
    half = len(tiles) // 2
    middle = LANES // 2
    low = lane_ids() < middle
    left = [jnp.where(low, tiles[i], pltpu.roll(tiles[i + half], middle, 1)) for i in range(half)]
    right = [jnp.where(low, pltpu.roll(tiles[i], middle, 1), tiles[i + half]) for i in range(half)]
    mine = [jnp.where(core == 0, a, b) for a, b in zip(left, right)]
    theirs = [jnp.where(core == 0, b, a) for a, b in zip(left, right)]
    return mine, theirs


def loosened(tiles):
    half = len(tiles)
    lane = lane_ids()
    natural = []
    for t in range(half):
        index = LANES // (2 * half) * t + lane // (2 * half) + LANES // 2 * (lane % (2 * half) // half)
        value = pick(tiles[0], index)
        for i in range(1, half):
            value = jnp.where(lane % half == i, pick(tiles[i], index), value)
        natural.append(value)
    return jnp.concatenate(natural, axis=1)


def arrange_fields(x_ref, *refs):
    own_ref, mate_ref = refs[-2:]
    half = x_ref.shape[3] // LANES
    for target, rows in zip((own_ref, mate_ref), both_rows()):
        for p in range(PARTS):
            natural = [x_ref[0, p, rows, t * LANES : (t + 1) * LANES] for t in range(half)]
            for i, tile in enumerate(compacted(natural)):
                target[p * half + i] = tile


def pack_block(mate, part_ref, other_ref, *refs):
    core = lax.axis_index("sub")
    block_ref = refs[-1]
    half = part_ref.shape[0] // PARTS
    rows = both_rows()[1 if mate else 0]
    for p in range(PARTS):
        mine = [part_ref[p * half + i] for i in range(half)]
        theirs = compacted([other_ref[0, p, rows, t * LANES : (t + 1) * LANES] for t in range(half)])
        left = [jnp.where(core == 0, x, y) for x, y in zip(mine, theirs)]
        right = [jnp.where(core == 0, y, x) for x, y in zip(mine, theirs)]
        for j, tile in enumerate(merged(left, right)):
            block_ref[2 * p * half + j] = tile


def pack_velocity(order_ref, *refs):
    slabs, (keep_ref, send_ref) = refs[:-3], refs[-2:]
    core = lax.axis_index("sub")
    here = lax.axis_index("freq")
    count = len(slabs)
    size = slabs[0].shape[0]
    half = keep_ref.shape[2] // LANES
    for target, row in ((keep_ref, core), (send_ref, 1 - core)):
        rows = pl.ds(pl.multiple_of(row * ROWS, ROWS), ROWS)
        for t in range(half):
            columns = slice(t * LANES, (t + 1) * LANES)
            values = [[slabs[s][i, rows, columns] for i in range(size)] for s in range(count)]
            for d in range(keep_ref.shape[0]):
                stored = order_ref[d]
                value = values[0][0]
                for s in range(count):
                    first = lax.rem(here + s, count) * size
                    for i in range(size):
                        if s or i:
                            value = jnp.where(stored == first + i, values[s][i], value)
                target[d, :, columns] = value


def chebyshev(terms, tiles, kcheb, up_scale, down_scale):
    lane = lane_ids()
    sub = lax.broadcasted_iota(jnp.int32, (ROWS, LANES), 0)
    first = lane == 0
    last = lane == LANES - 1
    half = ROWS // 2
    inside = jnp.full((ROWS, LANES), 0.25, jnp.float32)
    upper = jnp.where(sub < half, up_scale, inside)
    lower = jnp.where(sub >= half, down_scale, inside)
    own = 2 * ROWS
    for k in range(kcheb):
        reach = kcheb - (k + 1)
        if reach > half:
            windows = ((own - ROWS, up_scale), (own, inside), (own + ROWS, down_scale))
        elif reach > 0:
            windows = ((own - half, upper), (own + half, lower))
        else:
            windows = ((own, inside),)
        for row, scale in windows:
            for p in range(PARTS):
                base = p * tiles
                twice = []
                sums = []
                for j in range(tiles):
                    value = terms[k, base + j, pl.ds(row, ROWS), :]
                    double = value + value
                    around = terms[k, base + j, pl.ds(row - 1, ROWS), :] + terms[k, base + j, pl.ds(row + 1, ROWS), :]
                    sums.append(around + double)
                    twice.append(value if k == 0 else double)
                before = jnp.where(first, 0.0, pltpu.roll(sums[tiles - 1], 1, 1))
                after = jnp.where(last, 0.0, pltpu.roll(sums[0], LANES - 1, 1))
                pair = [sums[j] + sums[j + 1] for j in range(tiles - 1)]
                full = [pair[0] + (sums[0] + before)]
                full += [pair[j - 1] + pair[j] for j in range(1, tiles - 1)]
                full.append(pair[tiles - 2] + (sums[tiles - 1] + after))
                for j in range(tiles):
                    if k == 0:
                        new = (0.5 * scale) * full[j] - twice[j]
                    else:
                        new = scale * full[j] - (twice[j] + terms[k - 1, base + j, pl.ds(row, ROWS), :])
                    terms[k + 1, base + j, pl.ds(row, ROWS), :] = new


def bins_of(depth, bins, keep_ref, other_ref, tiles):
    core = lax.axis_index("sub")
    half = tiles // 2
    velocity = [None] * tiles
    for ref, home in ((keep_ref, core), (other_ref, 1 - core)):
        strips = [ref[depth, :, t * LANES : (t + 1) * LANES] for t in range(half)]
        velocity = spread_half(strips, home, velocity, tiles)
    lows = [jnp.clip(v.astype(jnp.int32), 0, bins - 1) for v in velocity]
    return lows, [v - low.astype(jnp.float32) for v, low in zip(velocity, lows)]


def coefficients(depth, bins, table_ref, keep_ref, other_ref, *refs):
    out_ref = refs[-1]
    count, tiles = out_ref.shape[:2]
    lows, parts = bins_of(depth, bins, keep_ref, other_ref, tiles)
    table = table_ref[...]
    step = pltpu.roll(table, LANES - 1, 1) - table
    for i in range(count):
        at_low = jnp.broadcast_to(table[i : i + 1], (ROWS, LANES))
        rise = jnp.broadcast_to(step[i : i + 1], (ROWS, LANES))
        for j in range(tiles):
            out_ref[i, j] = pick(at_low, lows[j]) + parts[j] * pick(rise, lows[j])


def combined(terms, coefficient, j, tiles, kcheb):
    own = 2 * ROWS
    total = None
    for k in range(kcheb + 1):
        a = coefficient(2 * k, j)
        b = coefficient(2 * k + 1, j)
        sr, si, rr, ri = [terms[k, p * tiles + j, pl.ds(own, ROWS), :] for p in range(PARTS)]
        adds = (a * sr + b * si, a * si - b * sr, a * rr - b * ri, a * ri + b * rr)
        total = adds if total is None else tuple(y + x for x, y in zip(adds, total))
    return total


def halves(stack, core):
    natural = straightened(stack)
    half = len(natural) // 2
    left, right = natural[:half], natural[half:]
    mine = [jnp.where(core == 0, a, b) for a, b in zip(left, right)]
    theirs = [jnp.where(core == 0, b, a) for a, b in zip(left, right)]
    return jnp.concatenate(mine, axis=1), jnp.concatenate(theirs, axis=1)


def depth_step(kcheb, bins, first, final, *refs):
    core = lax.axis_index("sub")
    block = lax.axis_index("lat") * 2 + core
    blocks = 2 * lax.axis_size("lat")
    refs, terms, lookup = refs[:-2], refs[-2], refs[-1]
    tiles = terms.shape[1] // PARTS
    if first:
        (table_ref, keep_ref, other_ref), refs = refs[:3], refs[3:]
        table = table_ref[...]
        step = pltpu.roll(table, LANES - 1, 1) - table
        for i in range(2 * (kcheb + 1)):
            lookup[0, i] = jnp.broadcast_to(table[i : i + 1], (ROWS, LANES))
            lookup[1, i] = jnp.broadcast_to(step[i : i + 1], (ROWS, LANES))
        lows, between = bins_of(0, bins, keep_ref, other_ref, tiles)

        def coefficient(i, j):
            return pick(lookup[0, i], lows[j]) + between[j] * pick(lookup[1, i], lows[j])
    else:
        ready, refs = refs[0], refs[1:]

        def coefficient(i, j):
            return ready[i, j]

    own = 2 * ROWS
    up_ok = block > 0
    down_ok = block < blocks - 1
    sources, refs = refs[:3], refs[3:]
    for i in range(PARTS * tiles):
        mine, a, b = [source[i] for source in sources]
        terms[0, i, pl.ds(own, ROWS), :] = mine
        terms[0, i, pl.ds(own - ROWS, ROWS), :] = jnp.where(up_ok, jnp.where(core == 0, b, a), 0.0)
        terms[0, i, pl.ds(own + ROWS, ROWS), :] = jnp.where(down_ok, jnp.where(core == 0, a, b), 0.0)
    shape = (ROWS, LANES)
    up_scale = jnp.where(up_ok, jnp.full(shape, 0.25, jnp.float32), 0.0)
    down_scale = jnp.where(down_ok, jnp.full(shape, 0.25, jnp.float32), 0.0)
    chebyshev(terms, tiles, kcheb, up_scale, down_scale)
    result = [combined(terms, coefficient, j, tiles, kcheb) for j in range(tiles)]
    images = [sr * rr + si * ri for sr, si, rr, ri in result]
    if not final:
        new_ref, image_ref = refs
        for j in range(tiles):
            for p in range(PARTS):
                new_ref[p * tiles + j] = result[j][p]
            image_ref[j] = images[j]
        return
    fields_ref, send_ref, here_ref, image_ref = refs[1:]
    half = tiles // 2
    for i, (mine, theirs) in enumerate(zip(*parted(images, core))):
        here_ref[i] = mine
        image_ref[i] = theirs
    for p in range(PARTS):
        for i, (mine, theirs) in enumerate(zip(*parted([total[p] for total in result], core))):
            fields_ref[p * half + i] = mine
            send_ref[p * half + i] = theirs


def early_images(*refs):
    past, (kept_ref, sub_ref, here_ref, cross_ref) = refs[:-5], refs[-4:]
    core = lax.axis_index("sub")
    owners = lax.axis_size("freq")
    here = lax.axis_index("freq")
    each = kept_ref.shape[0]
    empty = jnp.zeros(kept_ref.shape[1:], jnp.float32)
    for depth in range(len(past) + 1):
        if depth < len(past):
            mine, theirs = halves([past[depth][j] for j in range(past[depth].shape[0])], core)
        else:
            mine = theirs = empty
        shift = lax.rem(depth // each - here + owners, owners)
        slot = depth % each

        @pl.when(shift == 0)
        def _():
            kept_ref[slot] = mine
            sub_ref[slot] = theirs

        @pl.when(shift != 0)
        def _():
            here_ref[shift - 1, slot] = mine
            cross_ref[shift - 1, slot] = theirs


def both_rows():
    core = lax.axis_index("sub")
    return [pl.ds(pl.multiple_of(c * ROWS, ROWS), ROWS) for c in (core, 1 - core)]


def assemble_fields(own_ref, got_ref, fields_ref):
    half = own_ref.shape[0] // PARTS
    for rows, ref in zip(both_rows(), (own_ref, got_ref)):
        for p in range(PARTS):
            fields_ref[0, p, rows, :] = loosened([ref[p * half + i] for i in range(half)])


def assemble_images(count, *refs):
    early, late, image_ref = refs[: 2 * count], refs[2 * count : 4 * count], refs[-1]
    each = image_ref.shape[0]
    holds_last = lax.axis_index("freq") == lax.axis_size("freq") - 1
    for side, rows in enumerate(both_rows()):
        for d in range(each):
            value = functools.reduce(jnp.add, [r[d] for r in early[side::2]])
            if d == each - 1:
                half = late[0].shape[0]
                last = [functools.reduce(jnp.add, [r[i] for r in late[side::2]]) for i in range(half)]
                value = value + jnp.where(holds_last, loosened(last), 0.0)
            image_ref[d, rows, :] = value


def body(wavefields, velocity, filter_table, freq_pick, slab_order):
    f32 = jnp.float32
    lat = lax.axis_size("lat")
    freq = lax.axis_size("freq")
    bins, _, terms, _ = filter_table.shape
    kcheb = terms - 1
    _, parts, rows, cols = wavefields.shape
    depths = slab_order.shape[0]
    tiles = 2 * cols // LANES
    each = depths // freq
    assert rows == 2 * ROWS and kcheb == ROWS and parts == PARTS and lax.axis_size("sub") == 2

    def call(kernel, outs, args, params=SMALL, specs=None, scratch=(), flops=1 << 20):
        return pl.pallas_call(
            kernel,
            out_shape=tuple(jax.ShapeDtypeStruct(o, f32) for o in outs),
            in_specs=vmem(len(args)) if specs is None else specs,
            out_specs=tuple(vmem(len(outs))),
            scratch_shapes=scratch,
            compiler_params=params,
            cost_estimate=cost(flops),
        )(*args)

    def shifted(value, s):
        return lax.ppermute(value, "freq", [(i, (i + s) % freq) for i in range(freq)])

    def crossed(value, s):
        pairs = [(2 * i + c, 2 * ((i + s) % freq) + 1 - c) for i in range(freq) for c in range(2)]
        return lax.ppermute(value, ("freq", "sub"), pairs)

    slabs = [velocity]
    for s in range(1, freq):
        slabs.append(lax.ppermute(velocity, "freq", [((i + s) % freq, i) for i in range(freq)]))

    table = lax.dynamic_index_in_dim(filter_table, freq_pick[0], 1, keepdims=False)
    table = table.reshape(bins, 2 * terms).T
    table = jnp.pad(table, ((0, 0), (0, LANES - bins)))
    order = jnp.broadcast_to(slab_order[:, None, None], (depths, ROWS, LANES))

    chain = chain_permutation(lax.axis_size("shots"), lat, freq)
    axes = ("shots", "lat", "freq", "sub")
    compact = (PARTS * tiles // 2, ROWS, LANES)
    block = (PARTS * tiles, ROWS, LANES)
    other = lax.ppermute(wavefields, "sub", SWAP)
    own_part, mate_part = call(arrange_fields, (compact, compact), (wavefields,))
    own = call(functools.partial(pack_block, False), (block,), (own_part, other))[0]
    zmate = lax.ppermute(own, axes, chain)
    mate = call(functools.partial(pack_block, True), (block,), (mate_part, other, own))[0]

    strip = (depths, ROWS, cols)
    keep, send = call(pack_velocity, (strip, strip), (order, *slabs, mate))
    theirs = lax.ppermute(send, "sub", SWAP)

    def coefficients_of(depth, after):
        return call(
            functools.partial(coefficients, depth, bins),
            ((2 * terms, tiles, ROWS, LANES),),
            (table, keep, theirs) + after,
        )[0]

    scratch = [
        pltpu.VMEM((terms, PARTS * tiles, 5 * ROWS, LANES), f32),
        pltpu.VMEM((2, 2 * terms, ROWS, LANES), f32),
    ]
    ready = [(table, keep, theirs)] + [None] * (depths - 1)
    state = (own, mate, zmate)
    images = []
    for depth in range(depths - 1):
        own, image = call(
            functools.partial(depth_step, kcheb, bins, depth == 0, False),
            (block, (tiles, ROWS, LANES)),
            (*ready[depth], *state),
            params=STEP,
            scratch=scratch,
        )
        images.append(image)
        zmate = lax.ppermute(own, axes, chain)
        mate = lax.ppermute(own, "sub", SWAP)
        state = (own, mate, zmate)
        wanted = [depth + 1] if depth + 1 < depths - 1 else []
        if depth == max(depths - 3, 0):
            wanted.append(depths - 1)
        for d in wanted:
            ready[d] = (coefficients_of(d, (own,)),)

    row = (each, ROWS, cols)
    outs = (row, row, (freq - 1,) + row, (freq - 1,) + row)
    kept, sub_send, here_send, cross_send = call(early_images, outs, (*images, *ready[-1]))
    early = [kept, lax.ppermute(sub_send, "sub", SWAP)]
    for s in range(1, freq):
        early.append(shifted(here_send[s - 1], s))
        early.append(crossed(cross_send[s - 1], s))

    part = (tiles // 2, ROWS, LANES)
    fields, send, here, image_send = call(
        functools.partial(depth_step, kcheb, bins, depths == 1, True),
        (compact, compact, part, part),
        (*ready[-1], *state, kept),
        params=STEP,
        scratch=scratch,
    )
    image_got = lax.ppermute(image_send, "sub", SWAP)
    got = lax.ppermute(send, "sub", SWAP)
    late = [here, image_got]
    for s in range(1, freq):
        late.append(shifted(here, s))
        late.append(crossed(image_send, s))
    fields = call(assemble_fields, (wavefields.shape,), (fields, got))[0]
    image = call(functools.partial(assemble_images, freq), ((each, rows, cols),), (*early, *late))[0]
    return fields, image


def solution(mesh):
    return jax.shard_map(
        body,
        mesh=mesh,
        in_specs=(
            P(("shots", "freq"), None, "lat", "sub"),
            P("freq", "lat", "sub"),
            P(),
            P("freq"),
            P(),
        ),
        out_specs=(P(("shots", "freq"), None, "lat", "sub"), P(("shots", "freq"), "lat", "sub")),
        check_vma=False,
    )
```
